32 devices in a mesh: parts: 2 (over x), rows: 16 (over z, y, core).
Axes of the slice: x: 2, y: 2, z: 4, core: 2. Of those that a mesh axis runs over, the one named last changes fastest.
Arguments:
- traces: bfloat16 [16, 4096, 2048], P('parts', 'rows'), parts along dimension 0, may hold values from -6 to 6
- offset_bin: int32 [16, 4096], P('parts', 'rows'), parts along dimension 0, may hold values from 0 to 15
- filters: float32 [16, 32], replicated, may hold values from -1 to 1
- data_matrix: bfloat16 [128, 2, 64, 4096], P('parts', None, 'rows'), parts along dimension 0, may hold values from -0.0625 to 0.0625
Outputs:
- multiples: bfloat16 [128, 2, 8, 64], P(('parts', 'rows')), parts along dimension 0
The draws below stay inside these ranges and needn't reach their ends.
There are 2 independent parts, one for each index of `parts`. The reference program is written for one: setup_inputs(seed, part) draws one part's arguments, and reference() takes and returns one part's arrays. A program takes and returns all parts, laid end to end along the dimension named above; an argument that names none is the same for every part. Nothing has to cross between parts.
All inputs are finite; a program needn't handle non-finite values.
Results may differ from the reference program's by a relative error of at most 0.0067.
Values may be sent and summed in bfloat16 or wider, within the bound.
No kernel may reach another device: no remote copies, remote signals or barrier semaphores. Data moves between devices by JAX's collectives and lax.ppermute only.
A program may use at most 128 MiB of HBM per device.

```python
import math
import jax
import jax.numpy as jnp
from jax import lax

NR = 4096
NT = 2048
NF = 64
FIRST = 64
TAPS = 32
BINS = 16
SHOTS = 8
RW = 64


def set_ends(entries, key, low, high):
    dims = entries.shape
    place = [jax.random.randint(jax.random.fold_in(key, axis), (), 0, dims[axis]) for axis in range(len(dims))]
    entries = entries.at[tuple(place)].set(low)
    longest = dims.index(max(dims))
    place[longest] = (place[longest] + 1) % dims[longest]
    return entries.at[tuple(place)].set(high)


def block_levels(key, dims, pieces, smallest, high):
    def one(position, shards_of):
        draws = jax.random.uniform(jax.random.fold_in(jax.random.fold_in(key, 6), position), (shards_of,), jnp.float32, smallest / len(pieces), high / len(pieces))
        return jnp.repeat(jnp.exp(draws), dims[position] // shards_of).reshape((-1,) + (1,) * (len(dims) - position - 1))

    loudness = one(*pieces[0])
    for cut in pieces[1:]:
        loudness = loudness * one(*cut)
    return loudness


def scatter_about(own_key, shape, scale, limit, pieces=(), kind=jnp.bfloat16):
    array = jax.random.normal(own_key, shape, jnp.float32) * scale
    if len(pieces) > 0:
        array = block_levels(own_key, shape, pieces, -0.22, 0.18) * array
    return jnp.clip(array, min=-limit, max=limit).astype(kind)


def setup_inputs(seed: int = 0, part: int = 0) -> dict:
    keys = jax.random.split(jax.random.key(seed), 5)
    part_keys = jax.random.split(jax.random.fold_in(keys[4], part), 5)
    traces = scatter_about(part_keys[0], (SHOTS, NR, NT), 1.0, 6.0, ((1, 16),))
    offset_bin = set_ends(jax.random.randint(part_keys[1], (SHOTS, NR), 0, BINS), jax.random.fold_in(part_keys[1], 1), 0, BINS - 1).astype(jnp.int32)
    filters = scatter_about(keys[2], (BINS, TAPS), TAPS ** -0.5, 1.0, (), jnp.float32)
    data_matrix = scatter_about(part_keys[3], (NF, 2, RW, NR), (2 * NR) ** -0.5, 0.0625, ((2, 16),))
    return {"traces": traces, "offset_bin": offset_bin, "filters": filters, "data_matrix": data_matrix}


def spectral_table(freq_count, first_index, length):
    freq_index = first_index + jnp.arange(freq_count, dtype=jnp.int32)
    sample_index = jnp.arange(length, dtype=jnp.int32)
    product_index = freq_index[:, None] * sample_index[None, :] % length
    phase_angle = product_index.astype(jnp.float32) * jnp.float32(2.0 * math.pi / length)
    norm_factor = jnp.float32(1.0 / math.sqrt(length))
    stacked = jnp.stack([jnp.cos(phase_angle), -jnp.sin(phase_angle)], axis=1) * norm_factor
    return stacked.astype(jnp.bfloat16)

def reference(traces, offset_bin, filters, data_matrix):
    table = spectral_table(NF, FIRST, NT).reshape(2 * NF, NT)

    def one_shot(inputs):
        shot_traces, shot_bins = inputs
        tap_rows = filters[shot_bins]
        padded = jnp.pad(shot_traces, ((0, 0), (TAPS - 1, 0)))
        filtered = jnp.zeros((NR, NT), jnp.float32)
        for delay_index in range(TAPS):
            window = padded[:, TAPS - 1 - delay_index:TAPS - 1 - delay_index + NT]
            filtered = filtered + tap_rows[:, delay_index:delay_index + 1] * window.astype(jnp.float32)
        filtered = filtered.astype(jnp.bfloat16)
        return jnp.dot(table, filtered.T, preferred_element_type=jnp.float32).astype(jnp.bfloat16)
    spectra = lax.map(one_shot, (traces, offset_bin))
    spectra = jnp.transpose(spectra.reshape(SHOTS, NF, 2, NR), (1, 2, 0, 3))

    def one_freq(inputs):
        matrix_rows, shot_columns = inputs
        matrix_rows = matrix_rows.astype(jnp.float32)
        shot_columns = shot_columns.astype(jnp.float32)
        highest = lax.Precision.HIGHEST
        real_part = jnp.einsum('rk,sk->sr', matrix_rows[0], shot_columns[0], precision=highest) - jnp.einsum('rk,sk->sr', matrix_rows[1], shot_columns[1], precision=highest)
        imag_part = jnp.einsum('rk,sk->sr', matrix_rows[0], shot_columns[1], precision=highest) + jnp.einsum('rk,sk->sr', matrix_rows[1], shot_columns[0], precision=highest)
        return jnp.stack([real_part, imag_part]).astype(jnp.bfloat16)
    return lax.map(one_freq, (data_matrix, spectra))
```

```python
import functools
import math

import jax
import jax.numpy as jnp
import numpy as np
from jax import lax
from jax.experimental import pallas as pl
from jax.experimental.pallas import tpu as pltpu
from jax.sharding import PartitionSpec as P

FIRST = 64
BAND = 16
F32 = jnp.float32
BF16 = jnp.bfloat16


def dot(a, b, dims=((1,), (0,)), **kw):
    return lax.dot_general(a, b, (dims, ((), ())), preferred_element_type=F32, **kw)


def split(x, parts):
    pieces = []
    for _ in range(parts):
        piece = x.astype(BF16)
        pieces.append(piece)
        x = x - piece.astype(F32)
    return pieces


def transform_tables(freqs, length, taps, bins, shots):
    bands = freqs // BAND
    order = FIRST + np.arange(freqs).reshape(bands, 1, BAND)
    t = np.arange(length)

    def wave(samples, norm):
        angle = 2.0 * np.pi * ((samples[:, None, None, None] * order) % length) / length
        re, im = np.cos(angle) * norm, -np.sin(angle) * norm
        plain = np.concatenate([re, im], axis=2).reshape(len(samples), -1)
        swapped = np.concatenate([im, re], axis=2).reshape(len(samples), -1)
        return plain, swapped

    norm = 1.0 / math.sqrt(length)
    plain, swapped = wave(t, norm)
    main = np.concatenate([plain, swapped], axis=1)
    main[length - taps :] = 0.0
    one, _ = wave(np.arange(taps), 1.0)
    one = one.reshape(taps, bands, 2, BAND)
    resp_a = np.concatenate([one[:, :, :1], one[:, :, :1]], axis=2).reshape(taps, -1)
    resp_b = np.concatenate([-one[:, :, 1:], one[:, :, 1:]], axis=2).reshape(taps, -1)
    resp = np.concatenate([resp_a, resp_b], axis=1)
    u = np.arange(taps)
    tail = np.zeros((taps, taps, 2 * freqs))
    for j in range(taps):
        live = u + j < taps
        tail[j, live] = plain[length - taps + u[live] + j]
    lanes = min(128, length)
    spread = np.zeros((lanes, taps * bins))
    spread[lanes - taps + np.repeat(u, bins), np.arange(taps * bins)] = 1.0
    pick = np.tile(np.eye(bins), (1, taps))
    return (
        jnp.asarray(main, BF16),
        jnp.asarray(resp, F32),
        jnp.asarray(tail.reshape(taps, -1), BF16),
        jnp.asarray(spread, BF16),
        jnp.asarray(pick, BF16),
    )


def spectra_kernel(bands, trace, bin_of, filt, main, resp, tail, spread, pick, out, select, last):
    shot = pl.program_id(0)
    bins, taps = filt.shape
    width = main.shape[1] // 2
    lanes = spread.shape[0]

    @pl.when(shot == 0)
    def _():
        table = dot(filt[...], resp[...], precision=lax.Precision.HIGHEST)
        for i, piece in enumerate(split(table, 3)):
            select[i * bins : (i + 1) * bins, : 2 * width] = piece
            if i:
                select[i * bins : (i + 1) * bins, 2 * width :] = jnp.zeros_like(pick)
            else:
                select[:bins, 2 * width :] = pick[...]
        high, low = split(filt[...], 2)
        for u in range(taps):
            cols = tail[:, u * width : (u + 1) * width]
            last[u * bins : (u + 1) * bins, :] = (dot(high, cols) + dot(low, cols)).astype(BF16)

    signal = trace[0]
    count = signal.shape[0]
    row = lax.broadcasted_iota(jnp.int32, (3 * bins, count), 0) % bins
    chosen = (bin_of[0] == row).astype(F32).astype(BF16)
    looked = dot(chosen, select[...], ((0,), (0,)))
    spectrum = dot(signal, main[...])
    ending = dot(signal[:, signal.shape[1] - lanes :], spread[...]) * looked[:, 2 * width :]
    value = (
        spectrum[:, :width] * looked[:, :width]
        + spectrum[:, width:] * looked[:, width : 2 * width]
        + dot(ending.astype(BF16), last[...])
    )
    chunk = width // bands
    per = width // chunk
    place = lax.broadcasted_iota(jnp.int32, (count, width), 1) // chunk
    for j in range(per):

        @pl.when(shot % per == j)
        def _():
            for band in range(bands):
                moved = value if band == j else pltpu.roll(value, ((j - band) * chunk) % width, 1)
                if j:
                    moved = jnp.where(place == j, moved, out[band].astype(F32))
                out[band] = moved.astype(BF16)


def spectra_of(traces, offset_bin, filters, freqs):
    shots, count, length = traces.shape
    bins, taps = filters.shape
    bands = freqs // BAND
    width = 2 * freqs
    tables = transform_tables(freqs, length, taps, bins, shots)
    whole = [pl.BlockSpec(x.shape, lambda s: (0, 0)) for x in (filters,) + tables]
    per = width // (2 * BAND)
    return pl.pallas_call(
        functools.partial(spectra_kernel, bands),
        grid=(shots,),
        in_specs=[
            pl.BlockSpec((1, count, length), lambda s: (s, 0, 0)),
            pl.BlockSpec((1, 1, count), lambda s: (s, 0, 0)),
        ]
        + whole,
        out_specs=pl.BlockSpec((bands, count, width), lambda s: (0, 0, s // per)),
        out_shape=jax.ShapeDtypeStruct((bands, count, shots * 2 * BAND), BF16),
        scratch_shapes=[
            pltpu.VMEM((3 * bins, 2 * width + taps * bins), BF16),
            pltpu.VMEM((taps * bins, width), BF16),
        ],
        compiler_params=pltpu.CompilerParams(vmem_limit_bytes=48 << 20),
        name="spectra",
    )(traces, offset_bin[:, None, :], filters, *tables)


def copy_kernel(_, source, target):
    target[...] = source[...]


def rows_for(data_matrix, starts, block):
    freqs, parts, rows, _ = data_matrix.shape
    number = starts.shape[0]
    if block % 128:
        pieces = [
            lax.dynamic_slice_in_dim(data_matrix, starts[i] * block, block, 3) for i in range(number)
        ]
        return jnp.concatenate(pieces, axis=3)
    shape = (freqs, parts, rows, block)
    return pl.pallas_call(
        copy_kernel,
        grid_spec=pltpu.PrefetchScalarGridSpec(
            num_scalar_prefetch=1,
            grid=(number,),
            in_specs=[pl.BlockSpec(shape, lambda i, s: (0, 0, 0, s[i]))],
            out_specs=pl.BlockSpec(shape, lambda i, s: (0, 0, 0, i)),
        ),
        out_shape=jax.ShapeDtypeStruct(shape[:3] + (number * block,), data_matrix.dtype),
        name="rows_for",
    )(starts, data_matrix)


def predict_kernel(members, slots, *refs):
    rows_in, spectra_in = refs[:members], refs[members : members + slots]
    mask_ref, fold_a, fold_b, out = refs[members + slots :]
    total = None
    matrix = jnp.concatenate([r[...] for r in rows_in], axis=2)
    depth = matrix.shape[-1]
    matrix = matrix.reshape(-1, depth)
    block = spectra_in[0].shape[1]
    for i in range(slots):
        term = dot(matrix[:, i * block : (i + 1) * block], spectra_in[i][0])
        total = term if total is None else total + term
    total = jnp.where(mask_ref[...] != 0, total, 0.0)
    high, low = split(total, 2)
    a = dot(high, fold_a[...]) + dot(low, fold_a[...])
    b = dot(high, fold_b[...]) + dot(low, fold_b[...])
    rows = rows_in[0].shape[2] * members
    lanes = a.shape[1]
    a = a.reshape(BAND, 2, rows, lanes)
    b = b.reshape(BAND, 2, rows, lanes)
    value = a[:, 0] + b[:, 1]
    dests = out.shape[0]
    value = value.reshape(dests, BAND // dests, rows, lanes)
    acc = value[:, 0]
    for i in range(1, BAND // dests):
        acc = acc + value[:, i]
    out[...] = acc.astype(out.dtype)


def predict(row_parts, spectra_parts, share):
    freqs, _, rows, depth = row_parts[0].shape
    bands, block, cols = spectra_parts[0].shape
    shots = cols // (2 * BAND)
    members, slots = len(row_parts), len(spectra_parts)
    all_rows = members * rows
    lanes = share * 2 * shots
    row_f = np.arange(BAND * 2 * all_rows) // (2 * all_rows)
    col_s, col_c, col_f = np.unravel_index(np.arange(cols), (shots, 2, BAND))
    mask = (row_f[:, None] == col_f[None, :]).astype(np.float32)
    fold_a = np.zeros((cols, share, 2, shots), np.float32)
    fold_b = np.zeros((cols, share, 2, shots), np.float32)
    index = np.arange(cols)
    fold_a[index, col_f % share, col_c, col_s] = 1.0
    fold_b[index, col_f % share, 1 - col_c, col_s] = np.where(col_c == 1, -1.0, 1.0)
    consts = (
        jnp.asarray(mask, F32),
        jnp.asarray(fold_a.reshape(cols, lanes), BF16),
        jnp.asarray(fold_b.reshape(cols, lanes), BF16),
    )
    dests = BAND // share
    return pl.pallas_call(
        functools.partial(predict_kernel, members, slots),
        grid=(bands,),
        in_specs=[pl.BlockSpec((BAND, 2, rows, depth), lambda q: (q, 0, 0, 0))] * members
        + [pl.BlockSpec((1, block, cols), lambda q: (q, 0, 0))] * slots
        + [pl.BlockSpec(x.shape, lambda q: (0, 0)) for x in consts],
        out_specs=pl.BlockSpec((dests, all_rows, lanes), lambda q: (q, 0, 0)),
        out_shape=jax.ShapeDtypeStruct((freqs // share, all_rows, lanes), BF16),
        compiler_params=pltpu.CompilerParams(vmem_limit_bytes=48 << 20),
        name="predict",
    )(*row_parts, *spectra_parts, *consts)


def ring_of(length):
    return list(range(0, length, 2)) + list(range(1, length, 2))[::-1]


def shards(devices, members, traces, offset_bin, filters, data_matrix):
    shot_count, block, length = traces.shape
    freqs, _, row_count, _ = data_matrix.shape
    lines = devices // members
    ring = ring_of(lines)
    after = {ring[i]: ring[(i + 1) % lines] for i in range(lines)}
    before = {b: a for a, b in after.items()}
    blocks = np.zeros((devices, members, lines), np.int32)
    for device in range(devices):
        line, member = divmod(device, members)
        for slot in range(lines):
            for m in range(members):
                blocks[device, m, slot] = line * members + (member ^ m)
            line = before[line]
    mine = jnp.asarray(blocks)[lax.axis_index("rows")]

    row_parts = [None] * members
    for m in list(range(2, members)) + [1, 0][-min(members, 2) :]:
        part = rows_for(data_matrix, mine[m], block)
        if m:
            part = lax.ppermute(part, "rows", [(i, i ^ m) for i in range(devices)])
        row_parts[m] = part

    spectra = spectra_of(traces, offset_bin, filters, freqs)
    spectra_parts = [spectra]
    step = [(i, after[i // members] * members + i % members) for i in range(devices)]
    for _ in range(lines - 1):
        spectra_parts.append(lax.ppermute(spectra_parts[-1], "rows", step))
    if block % 128:
        spectra_parts = [jnp.concatenate(spectra_parts, axis=1)]

    share = freqs // devices
    partial_value = predict(row_parts, spectra_parts, share)
    received = lax.all_to_all(partial_value, "rows", split_axis=0, concat_axis=0, tiled=True)
    choose = np.zeros((lines, members, members, row_count, lines, members, row_count))
    for line in range(lines):
        for member in range(members):
            for j in range(members):
                for r in range(row_count):
                    choose[line, member, member ^ j, r, line, j, r] = 1.0
    rows = devices * members * row_count
    choose = jnp.asarray(choose.reshape(rows, devices * row_count), BF16)
    final = dot(received.reshape(rows, -1), choose, ((0,), (0,)))
    return final.astype(BF16).reshape(share, 2, shot_count, devices * row_count)


def solution(mesh):
    devices = mesh.shape["rows"]
    members = math.gcd(devices, 4)
    in_specs = (P("parts", "rows", None), P("parts", "rows"), P(), P("parts", None, "rows", None))
    out_specs = P(("parts", "rows"), None, None, None)
    return jax.shard_map(
        functools.partial(shards, devices, members),
        mesh=mesh,
        in_specs=in_specs,
        out_specs=out_specs,
        check_vma=False,
    )
```

```python
import functools
import math

import jax
import jax.numpy as jnp
import numpy as np
from jax import lax
from jax.experimental import pallas as pl
from jax.experimental.pallas import tpu as pltpu
from jax.sharding import PartitionSpec as P


FIRST = 64
BAND = 16
F32 = jnp.float32
BF16 = jnp.bfloat16


def dot(a, b, dims=((1,), (0,)), **kw):
    return lax.dot_general(a, b, (dims, ((), ())), preferred_element_type=F32, **kw)


def split(x, parts):
    pieces = []
    for _ in range(parts):
        piece = x.astype(BF16)
        pieces.append(piece)
        x = x - piece.astype(F32)
    return pieces


def transform_tables(freqs, length, taps):
    bands = freqs // BAND
    order = FIRST + np.arange(freqs).reshape(bands, 1, BAND)
    lanes = 2 * freqs

    def wave(samples, norm):
        angle = 2.0 * np.pi * ((samples[:, None, None, None] * order) % length) / length
        re, im = np.cos(angle) * norm, -np.sin(angle) * norm
        plain = np.concatenate([re, im], axis=2).reshape(len(samples), -1)
        swapped = np.concatenate([im, re], axis=2).reshape(len(samples), -1)
        return plain, swapped

    plain, swapped = wave(np.arange(length), 1.0 / math.sqrt(length))
    main = np.concatenate([plain, swapped], axis=1)
    main[length - taps :] = 0.0
    one, _ = wave(np.arange(taps), 1.0)
    one = one.reshape(taps, bands, 2, BAND)
    resp_a = np.concatenate([one[:, :, :1], one[:, :, :1]], axis=2).reshape(taps, -1)
    resp_b = np.concatenate([-one[:, :, 1:], one[:, :, 1:]], axis=2).reshape(taps, -1)
    resp = np.concatenate([resp_a, resp_b], axis=1)
    u = np.arange(taps)
    tail = np.zeros((taps, taps, lanes))
    for j in range(taps):
        live = u + j < taps
        tail[j, live] = plain[length - taps + u[live] + j]
    return (
        jnp.asarray(main, BF16),
        jnp.asarray(resp, F32),
        jnp.asarray(tail.reshape(taps, -1), BF16),
    )


def spectra_kernel(
    bands, trace, bin_of, filt, main_hbm, resp_hbm, tail_hbm, out,
    main, resp, tail, select, last_rows, last, binned, sems,
):
    step = pl.program_id(0)
    bins, taps = filt.shape
    width = main.shape[1] // 2
    shots, count = bin_of.shape
    group, _, length = trace.shape
    copies = [
        pltpu.make_async_copy(a, b, sems.at[i])
        for i, (a, b) in enumerate(((main_hbm, main), (resp_hbm, resp), (tail_hbm, tail)))
    ]

    @pl.when(step == 0)
    def _():
        for copy in copies:
            copy.start()
        column = jnp.transpose(bin_of[...].astype(F32), (1, 0))
        for shot in range(shots):
            value = jnp.broadcast_to(column[:, shot : shot + 1], (count, width))
            binned[shot] = value.astype(BF16)
        copies[1].wait()
        copies[2].wait()
        table = dot(filt[...], resp[...], precision=lax.Precision.HIGHEST)
        select[...] = jnp.zeros_like(select)
        for i, piece in enumerate(split(table, 3)):
            select[i * bins : (i + 1) * bins, :] = piece
        high, low = split(filt[...], 2)
        for u in range(taps):
            cols = tail[:, u * width : (u + 1) * width]
            last_rows[pl.ds(u, bins, stride=taps), :] = dot(high, cols) + dot(low, cols)
        last[...] = last_rows[...].astype(BF16)
        copies[0].wait()

    signal = trace[...].reshape(group * count, length)
    of = binned[pl.ds(step * group, group)].reshape(group * count, width).astype(F32)
    lane = lax.broadcasted_iota(jnp.int32, (1, width), 1)
    lane_bin = jnp.where(lane < 3 * bins, lane % bins, -1).astype(F32)
    chosen = jnp.where(of == lane_bin, 1.0, 0.0).astype(BF16)
    looked = dot(chosen, select[...])
    ends = signal[:, length - width :].astype(F32)
    shift = taps
    while shift < width:
        ends = jnp.where(lane >= width - shift, ends, pltpu.roll(ends, width - shift, 1))
        shift *= 2
    every = width // taps
    ending = [
        jnp.where(of == (lane // taps + base).astype(F32), ends, 0.0).astype(BF16)
        for base in range(0, bins, every)
    ]
    ending = jnp.concatenate(ending, axis=1)
    spectrum = dot(signal, main[...])
    value = (
        spectrum[:, :width] * looked[:, :width]
        + spectrum[:, width:] * looked[:, width:]
        + dot(ending, last[...])
    )
    chunk = 2 * BAND
    per = width // chunk
    place = lax.broadcasted_iota(jnp.int32, (count, width), 1) // chunk
    for phase in range(max(per // group, 1)):

        @pl.when(step % max(per // group, 1) == phase)
        def _():
            moved = []
            for i in range(group):
                j = (phase * group + i) % per
                part = value[i * count : (i + 1) * count]
                moved.append(part if j == 0 else pltpu.roll(part, j * chunk, 1))
            for band in range(bands):
                result = moved[0] if phase == 0 else out[band].astype(F32)
                for i in range(group):
                    j = (phase * group + i) % per
                    if phase or i:
                        result = jnp.where(place == (band + j) % per, moved[i], result)
                out[band] = result.astype(BF16)


def chunk_of(shot, band, per):
    return shot // per * per + (band + shot % per) % per


def spectra_of(traces, offset_bin, filters, freqs):
    shots, count, length = traces.shape
    bins, taps = filters.shape
    bands = freqs // BAND
    width = 2 * freqs
    group = 2
    tables = transform_tables(freqs, length, taps)
    per = width // (2 * BAND)
    hbm = pl.BlockSpec(memory_space=pltpu.HBM)
    return pl.pallas_call(
        functools.partial(spectra_kernel, bands),
        grid=(shots // group,),
        in_specs=[
            pl.BlockSpec((group, count, length), lambda s: (s, 0, 0)),
            pl.BlockSpec((shots, count), lambda s: (0, 0)),
            pl.BlockSpec((bins, taps), lambda s: (0, 0)),
            hbm,
            hbm,
            hbm,
        ],
        out_specs=pl.BlockSpec((bands, count, width), lambda s: (0, 0, s * group // per)),
        out_shape=jax.ShapeDtypeStruct((bands, count, shots * 2 * BAND), BF16),
        scratch_shapes=[
            pltpu.VMEM(tables[0].shape, BF16),
            pltpu.VMEM(tables[1].shape, F32),
            pltpu.VMEM(tables[2].shape, BF16),
            pltpu.VMEM((width, 2 * width), BF16),
            pltpu.VMEM((taps * bins, width), F32),
            pltpu.VMEM((taps * bins, width), BF16),
            pltpu.VMEM((shots, count, width), BF16),
            pltpu.SemaphoreType.DMA((3,)),
        ],
        compiler_params=pltpu.CompilerParams(vmem_limit_bytes=56 << 20),
        cost_estimate=pl.CostEstimate(
            flops=2 * shots * count * length * 2 * width,
            bytes_accessed=traces.size * 2,
            transcendentals=0,
        ),
        name="spectra",
    )(traces, offset_bin, filters, *tables)


def rows_kernel(block, head, starts, source, first, rest, buffer, in_sems, out_sems):
    slots = buffer.shape[1]
    bands = buffer.shape[0]
    ins = []
    device = lax.axis_index("rows")
    for i in range(slots):
        start = jnp.int32(0)
        for d, row in enumerate(starts):
            start = jnp.where(device == d, jnp.int32(int(row[i]) * block), start)
        column = pl.multiple_of(start, block)
        ins.append(
            pltpu.make_async_copy(
                source.at[:, :, :, :, pl.ds(column, block)], buffer.at[:, i], in_sems.at[i]
            )
        )
        ins[-1].start()
    outs = []
    for i in range(slots):
        ins[i].wait()
        for k, (low, high, target) in enumerate(((0, head, first), (head, bands, rest))):
            copy = pltpu.make_async_copy(
                buffer.at[low:high, i], target.at[:, i], out_sems.at[i, k]
            )
            copy.start()
            outs.append(copy)
    for copy in outs:
        copy.wait()


def rows_for(data_matrix, starts, block, head):
    freqs, parts, rows, _ = data_matrix.shape
    bands = freqs // BAND
    slots = starts.shape[1]
    source = data_matrix.reshape(bands, BAND, parts, rows, -1)
    if block % 128:
        starts = jnp.asarray(starts)[lax.axis_index("rows")]
        pieces = [
            lax.dynamic_slice_in_dim(source, starts[i] * block, block, 4) for i in range(slots)
        ]
        both = jnp.stack(pieces, axis=1)
        return both[:head], both[head:]
    shape = (slots, BAND, parts, rows, block)
    kind = data_matrix.dtype
    return pl.pallas_call(
        functools.partial(rows_kernel, block, head, starts),
        in_specs=[pl.BlockSpec(memory_space=pltpu.HBM)],
        out_specs=[pl.BlockSpec(memory_space=pltpu.HBM)] * 2,
        out_shape=[
            jax.ShapeDtypeStruct((head,) + shape, kind),
            jax.ShapeDtypeStruct((bands - head,) + shape, kind),
        ],
        scratch_shapes=[
            pltpu.VMEM((bands,) + shape, kind),
            pltpu.SemaphoreType.DMA((slots,)),
            pltpu.SemaphoreType.DMA((slots, 2)),
        ],
        name="rows_for",
    )(source)


def predict_kernel(members, slots, *refs):
    rows_in, spectra_in = refs[:members], refs[members : members + slots]
    mask_ref, fold_a, fold_b, out = refs[members + slots :]
    columns = []
    for i in range(rows_in[0].shape[1]):
        part = jnp.concatenate([r[0, i] for r in rows_in], axis=2)
        columns.append(part.reshape(-1, part.shape[-1]))
    matrix = columns[0] if len(columns) == 1 else jnp.concatenate(columns, axis=1)
    spectra = [r[0] for r in spectra_in]
    spectra = spectra[0] if slots == 1 else jnp.concatenate(spectra, axis=0)
    rows = rows_in[0].shape[4] * members
    total = dot(matrix, spectra)
    total = total.reshape(BAND, 2, rows, -1)
    acc = None
    for c, fold in enumerate((fold_a, fold_b)):
        value = total[:, c].reshape(BAND * rows, -1)
        value = jnp.where(mask_ref[...] != 0, value, 0.0)
        for piece in split(value, 2):
            term = dot(piece, fold[0])
            acc = term if acc is None else acc + term
    dests = out.shape[0]
    acc = acc.reshape(dests, BAND // dests, rows, -1)
    value = acc[:, 0]
    for i in range(1, BAND // dests):
        value = value + acc[:, i]
    out[...] = value.astype(out.dtype)


def predict(row_parts, spectra_parts, share, first):
    number, pieces, _, _, rows, depth = row_parts[0].shape
    bands, block, cols = spectra_parts[0].shape
    shots = cols // (2 * BAND)
    per = 2 * BAND * bands // (2 * BAND)
    members, slots = len(row_parts), len(spectra_parts)
    all_rows = members * rows
    lanes = share * 2 * shots
    index = np.arange(cols)
    col_c, col_f = index // BAND % 2, index % BAND
    row_f = np.arange(BAND * all_rows) // all_rows
    mask = (row_f[:, None] == col_f[None, :]).astype(np.float32)
    fold_a = np.zeros((bands, cols, share, 2, shots), np.float32)
    fold_b = np.zeros((bands, cols, share, 2, shots), np.float32)
    for band in range(bands):
        shot_at = np.zeros(shots, np.int64)
        for shot in range(shots):
            shot_at[chunk_of(shot, band, per)] = shot
        col_s = shot_at[index // (2 * BAND)]
        fold_a[band, index, col_f % share, col_c, col_s] = 1.0
        fold_b[band, index, col_f % share, 1 - col_c, col_s] = np.where(col_c == 1, -1.0, 1.0)
    consts = (
        jnp.asarray(mask, F32),
        jnp.asarray(fold_a.reshape(bands, cols, lanes), BF16),
        jnp.asarray(fold_b.reshape(bands, cols, lanes), BF16),
    )
    dests = BAND // share
    return pl.pallas_call(
        functools.partial(predict_kernel, members, slots),
        grid=(number,),
        in_specs=[pl.BlockSpec((1, pieces, BAND, 2, rows, depth), lambda q: (q, 0, 0, 0, 0, 0))]
        * members
        + [pl.BlockSpec((1, block, cols), lambda q: (first + q, 0, 0))] * slots
        + [pl.BlockSpec(mask.shape, lambda q: (0, 0))]
        + [pl.BlockSpec((1, cols, lanes), lambda q: (first + q, 0, 0))] * 2,
        out_specs=pl.BlockSpec((dests, all_rows, lanes), lambda q: (q, 0, 0)),
        out_shape=jax.ShapeDtypeStruct((number * dests, all_rows, lanes), BF16),
        compiler_params=pltpu.CompilerParams(vmem_limit_bytes=48 << 20),
        name="predict",
    )(*row_parts, *spectra_parts, *consts)


def ring_of(length):
    return list(range(0, length, 2)) + list(range(1, length, 2))[::-1]


def shards(devices, members, traces, offset_bin, filters, data_matrix):
    shot_count, block, _ = traces.shape
    freqs, _, row_count, _ = data_matrix.shape
    lines = devices // members
    ring = ring_of(lines)
    after = {ring[i]: ring[(i + 1) % lines] for i in range(lines)}
    before = {b: a for a, b in after.items()}
    blocks = np.zeros((devices, members, lines), np.int32)
    for device in range(devices):
        line, member = divmod(device, members)
        for slot in range(lines):
            for m in range(members):
                blocks[device, m, slot] = line * members + (member ^ m)
            line = before[line]

    bands = freqs // BAND
    head = max(bands - 1, 1)
    first_parts, rest_parts = [None] * members, [None] * members

    def exchange(m):
        first, rest = rows_for(data_matrix, blocks[:, m], block, head)
        pairs = [(i, i ^ m) for i in range(devices)]
        if m:
            first = lax.ppermute(first, "rows", pairs)
            rest = lax.ppermute(rest, "rows", pairs)
        first_parts[m], rest_parts[m] = first, rest

    for m in range(members - 1, -1, -1):
        exchange(m)

    spectra = spectra_of(traces, offset_bin, filters, freqs)
    spectra_parts = [spectra]
    step = [(i, after[i // members] * members + i % members) for i in range(devices)]
    for _ in range(lines - 1):
        spectra_parts.append(lax.ppermute(spectra_parts[-1], "rows", step))
    if block % 128:
        spectra_parts = [jnp.concatenate(spectra_parts, axis=1)]
        joined = lambda x: jnp.concatenate([x[:, i : i + 1] for i in range(lines)], axis=5)
        first_parts = [joined(x) for x in first_parts]
        rest_parts = [joined(x) for x in rest_parts]

    share = freqs // devices
    early = predict(first_parts, spectra_parts, share, 0)
    late = predict(rest_parts, spectra_parts, share, head)
    partial_value = jnp.concatenate([early, late], axis=0)
    received = lax.all_to_all(partial_value, "rows", split_axis=0, concat_axis=0, tiled=True)
    choose = np.zeros((lines, members, members, row_count, lines, members, row_count))
    for line in range(lines):
        for member in range(members):
            for j in range(members):
                for r in range(row_count):
                    choose[line, member, member ^ j, r, line, j, r] = 1.0
    rows = devices * members * row_count
    choose = jnp.asarray(choose.reshape(rows, devices * row_count), BF16)
    final = dot(received.reshape(rows, -1), choose, ((0,), (0,)))
    return final.astype(BF16).reshape(share, 2, shot_count, devices * row_count)


def solution(mesh):
    devices = mesh.shape["rows"]
    members = math.gcd(devices, 4)
    in_specs = (P("parts", "rows", None), P("parts", "rows"), P(), P("parts", None, "rows", None))
    out_specs = P(("parts", "rows"), None, None, None)
    return jax.shard_map(
        functools.partial(shards, devices, members),
        mesh=mesh,
        in_specs=in_specs,
        out_specs=out_specs,
        check_vma=False,
    )
```

```python
import functools
import math

import jax
import jax.numpy as jnp
import numpy as np
from jax import lax
from jax.experimental import pallas as pl
from jax.experimental.pallas import tpu as pltpu
from jax.sharding import PartitionSpec as P


FIRST = 64
BAND = 16
F32 = jnp.float32
BF16 = jnp.bfloat16


def dot(a, b, dims=((1,), (0,)), **kw):
    return lax.dot_general(a, b, (dims, ((), ())), preferred_element_type=F32, **kw)


def split(x, parts):
    pieces = []
    for _ in range(parts):
        piece = x.astype(BF16)
        pieces.append(piece)
        x = x - piece.astype(F32)
    return pieces


def transform_tables(freqs, length, taps):
    bands = freqs // BAND
    order = FIRST + np.arange(freqs).reshape(bands, 1, BAND)
    lanes = 2 * freqs

    def wave(samples, norm):
        angle = 2.0 * np.pi * ((samples[:, None, None, None] * order) % length) / length
        re, im = np.cos(angle) * norm, -np.sin(angle) * norm
        plain = np.concatenate([re, im], axis=2).reshape(len(samples), -1)
        swapped = np.concatenate([im, re], axis=2).reshape(len(samples), -1)
        return plain, swapped

    plain, swapped = wave(np.arange(length), 1.0 / math.sqrt(length))
    main = np.concatenate([plain, swapped], axis=1)
    main[length - taps :] = 0.0
    one, _ = wave(np.arange(taps), 1.0)
    one = one.reshape(taps, bands, 2, BAND)
    resp_a = np.concatenate([one[:, :, :1], one[:, :, :1]], axis=2).reshape(taps, -1)
    resp_b = np.concatenate([-one[:, :, 1:], one[:, :, 1:]], axis=2).reshape(taps, -1)
    resp = np.concatenate([resp_a, resp_b], axis=1)
    tail = np.zeros((lanes, lanes))
    tail[:taps] = plain[length - taps :]
    return jnp.asarray(main, BF16), jnp.asarray(resp, F32), jnp.asarray(tail, BF16)


def prepare(bins, taps, width, filt, resp, tail, select, last):
    filt_parts, resp_parts = split(filt[...], 2), split(resp[...], 2)
    table = dot(
        jnp.concatenate([filt_parts[0], filt_parts[1], filt_parts[0]], axis=1),
        jnp.concatenate([resp_parts[0], resp_parts[0], resp_parts[1]], axis=0),
    )
    select[...] = jnp.zeros_like(select)
    for i, piece in enumerate(split(table, 2)):
        select[i * bins : (i + 1) * bins, :] = piece
    rows = []
    for b in range(bins):
        row = jnp.pad(filt[b : b + 1, :], ((0, 0), (0, width - taps)))
        row = jnp.broadcast_to(row, (taps, width))
        rows.append(pltpu.roll(row, 0, 1, stride=1, stride_axis=0))
    rows = jnp.concatenate(rows, axis=0)
    high, low = split(rows, 2)
    last[...] = (dot(high, tail[...]) + dot(low, tail[...])).astype(BF16)


def chunk_of(shot, band, per):
    return shot // per * per + (band + shot % per) % per


def spectra_kernel(bands, bins, taps, first, *refs):
    trace, bin_of, main_hbm = refs[:3]
    if first:
        filt, resp, tail, out, select, last, main, binned, sem = refs[3:]
    else:
        select, last, out, main, binned, sem = refs[3:]
    step = pl.program_id(0)
    width = main.shape[1] // 2
    shots, count = bin_of.shape[1:]
    group, _, length = trace.shape
    copy = pltpu.make_async_copy(main_hbm, main, sem)

    @pl.when(step == 0)
    def _():
        copy.start()
        column = jnp.transpose(bin_of[0].astype(F32), (1, 0))
        for shot in range(shots):
            value = jnp.broadcast_to(column[:, shot : shot + 1], (count, width))
            binned[shot] = value.astype(BF16)
        if first:
            prepare(bins, taps, width, filt, resp, tail, select, last)
        copy.wait()

    signal = trace[...].reshape(group * count, length)
    of = binned[pl.ds(step * group, group)].reshape(group * count, width).astype(F32)
    lane = lax.broadcasted_iota(jnp.int32, (1, width), 1)
    lane_bin = jnp.where(lane < 2 * bins, lane % bins, -1).astype(F32)
    chosen = jnp.where(of == lane_bin, 1.0, 0.0).astype(BF16)
    looked = dot(chosen, select[...])
    ends = signal[:, length - width :].astype(F32)
    shift = taps
    while shift < width:
        ends = jnp.where(lane >= width - shift, ends, pltpu.roll(ends, width - shift, 1))
        shift *= 2
    every = width // taps
    ending = [
        jnp.where(of == (lane // taps + base).astype(F32), ends, 0.0).astype(BF16)
        for base in range(0, bins, every)
    ]
    ending = jnp.concatenate(ending, axis=1)
    spectrum = dot(signal, main[...])
    value = (
        spectrum[:, :width] * looked[:, :width]
        + spectrum[:, width:] * looked[:, width:]
        + dot(ending, last[...])
    )
    chunk = 2 * BAND
    per = width // chunk
    place = lax.broadcasted_iota(jnp.int32, (count, width), 1) // chunk
    for phase in range(per // group):

        @pl.when(step == phase)
        def _():
            moved = []
            for i in range(group):
                j = phase * group + i
                part = value[i * count : (i + 1) * count]
                moved.append(part if j == 0 else pltpu.roll(part, j * chunk, 1))
            for band in range(bands):
                result = moved[0] if phase == 0 else out[band].astype(F32)
                for i in range(group):
                    j = phase * group + i
                    if j:
                        result = jnp.where(place == (band + j) % per, moved[i], result)
                out[band] = result.astype(BF16)


def spectra_of(traces, offset_bin, filters, freqs):
    shots, count, length = traces.shape
    bins, taps = filters.shape
    bands = freqs // BAND
    width = 2 * freqs
    group = 2
    main, resp, tail = transform_tables(freqs, length, taps)
    per = width // (2 * BAND)
    out_shape = jax.ShapeDtypeStruct((bands, count, width), BF16)
    made = [
        jax.ShapeDtypeStruct((width, 2 * width), BF16),
        jax.ShapeDtypeStruct((taps * bins, width), BF16),
    ]
    whole = lambda x: pl.BlockSpec(x.shape, lambda s: (0,) * len(x.shape))
    binned = offset_bin.reshape(shots // per, per, count)
    results, extra = [], None
    for part in range(shots // per):
        first = part == 0
        more = [filters, resp, tail] if first else extra
        outs = pl.pallas_call(
            functools.partial(spectra_kernel, bands, bins, taps, first),
            grid=(per // group,),
            in_specs=[
                pl.BlockSpec(
                    (group, count, length),
                    functools.partial(lambda p, s: (p + s, 0, 0), part * per // group),
                ),
                pl.BlockSpec((1, per, count), functools.partial(lambda p, s: (p, 0, 0), part)),
                pl.BlockSpec(memory_space=pltpu.HBM),
            ]
            + [whole(x) for x in more],
            out_specs=[whole(out_shape)] + ([whole(x) for x in made] if first else []),
            out_shape=[out_shape] + (made if first else []),
            scratch_shapes=[
                pltpu.VMEM(main.shape, BF16),
                pltpu.VMEM((per, count, width), BF16),
                pltpu.SemaphoreType.DMA,
            ],
            compiler_params=pltpu.CompilerParams(vmem_limit_bytes=60 << 20),
            cost_estimate=pl.CostEstimate(
                flops=2 * per * count * length * 2 * width,
                bytes_accessed=per * count * length * 2,
                transcendentals=0,
            ),
            name="spectra",
        )(traces, binned, main, *more)
        if first:
            extra = outs[1:]
        results.append(outs[0])
    return results


def rows_kernel(block, head, starts, source, first, rest, buffer, in_sems, out_sems):
    slots = buffer.shape[1]
    bands = buffer.shape[0]
    ins = []
    device = lax.axis_index("rows")
    for i in range(slots):
        start = jnp.int32(0)
        for d, row in enumerate(starts):
            start = jnp.where(device == d, jnp.int32(int(row[i]) * block), start)
        column = pl.multiple_of(start, block)
        ins.append(
            pltpu.make_async_copy(
                source.at[:, :, :, :, pl.ds(column, block)], buffer.at[:, i], in_sems.at[i]
            )
        )
        ins[-1].start()
    outs = []
    for i in range(slots):
        ins[i].wait()
        for k, (low, high, target) in enumerate(((0, head, first), (head, bands, rest))):
            copy = pltpu.make_async_copy(
                buffer.at[low:high, i], target.at[:, i], out_sems.at[i, k]
            )
            copy.start()
            outs.append(copy)
    for copy in outs:
        copy.wait()


def rows_for(data_matrix, starts, block, head):
    freqs, parts, rows, _ = data_matrix.shape
    bands = freqs // BAND
    slots = starts.shape[1]
    source = data_matrix.reshape(bands, BAND, parts, rows, -1)
    if block % 128:
        starts = jnp.asarray(starts)[lax.axis_index("rows")]
        pieces = [
            lax.dynamic_slice_in_dim(source, starts[i] * block, block, 4) for i in range(slots)
        ]
        both = jnp.stack(pieces, axis=1)
        return both[:head], both[head:]
    shape = (slots, BAND, parts, rows, block)
    kind = data_matrix.dtype
    return pl.pallas_call(
        functools.partial(rows_kernel, block, head, starts),
        in_specs=[pl.BlockSpec(memory_space=pltpu.HBM)],
        out_specs=[pl.BlockSpec(memory_space=pltpu.HBM)] * 2,
        out_shape=[
            jax.ShapeDtypeStruct((head,) + shape, kind),
            jax.ShapeDtypeStruct((bands - head,) + shape, kind),
        ],
        scratch_shapes=[
            pltpu.VMEM((bands,) + shape, kind),
            pltpu.SemaphoreType.DMA((slots,)),
            pltpu.SemaphoreType.DMA((slots, 2)),
        ],
        name="rows_for",
    )(source)


def predict_kernel(members, slots, parts, *refs):
    rows_in, spectra_in = refs[:members], refs[members : members + slots * parts]
    mask_ref, fold_a, fold_b, out = refs[members + slots * parts :]
    columns = []
    for i in range(rows_in[0].shape[1]):
        part = jnp.concatenate([r[0, i] for r in rows_in], axis=2)
        columns.append(part.reshape(-1, part.shape[-1]))
    matrix = columns[0] if len(columns) == 1 else jnp.concatenate(columns, axis=1)
    spectra = [
        jnp.concatenate([spectra_in[p * slots + i][0] for p in range(parts)], axis=1)
        for i in range(slots)
    ]
    spectra = spectra[0] if slots == 1 else jnp.concatenate(spectra, axis=0)
    rows = rows_in[0].shape[4] * members
    total = dot(matrix, spectra)
    total = total.reshape(BAND, 2, rows, -1)
    acc = None
    for c, fold in enumerate((fold_a, fold_b)):
        value = total[:, c].reshape(BAND * rows, -1)
        value = jnp.where(mask_ref[...] != 0, value, 0.0)
        for piece in split(value, 2):
            term = dot(piece, fold[0])
            acc = term if acc is None else acc + term
    dests = out.shape[0]
    acc = acc.reshape(dests, BAND // dests, rows, -1)
    value = acc[:, 0]
    for i in range(1, BAND // dests):
        value = value + acc[:, i]
    out[...] = value.astype(out.dtype)


def predict(row_parts, spectra_parts, share, first):
    number, pieces, _, _, rows, depth = row_parts[0].shape
    parts, slots = len(spectra_parts), len(spectra_parts[0])
    bands, block, width = spectra_parts[0][0].shape
    cols = width * parts
    shots = cols // (2 * BAND)
    per = width // (2 * BAND)
    members = len(row_parts)
    all_rows = members * rows
    lanes = share * 2 * shots
    index = np.arange(cols)
    col_c, col_f = index // BAND % 2, index % BAND
    row_f = np.arange(BAND * all_rows) // all_rows
    mask = (row_f[:, None] == col_f[None, :]).astype(np.float32)
    fold_a = np.zeros((bands, cols, share, 2, shots), np.float32)
    fold_b = np.zeros((bands, cols, share, 2, shots), np.float32)
    for band in range(bands):
        shot_at = np.zeros(shots, np.int64)
        for shot in range(shots):
            shot_at[chunk_of(shot, band, per)] = shot
        col_s = shot_at[index // (2 * BAND)]
        fold_a[band, index, col_f % share, col_c, col_s] = 1.0
        fold_b[band, index, col_f % share, 1 - col_c, col_s] = np.where(col_c == 1, -1.0, 1.0)
    consts = (
        jnp.asarray(mask, F32),
        jnp.asarray(fold_a.reshape(bands, cols, lanes), BF16),
        jnp.asarray(fold_b.reshape(bands, cols, lanes), BF16),
    )
    dests = BAND // share
    return pl.pallas_call(
        functools.partial(predict_kernel, members, slots, parts),
        grid=(number,),
        in_specs=[pl.BlockSpec((1, pieces, BAND, 2, rows, depth), lambda q: (q, 0, 0, 0, 0, 0))]
        * members
        + [pl.BlockSpec((1, block, width), lambda q: (first + q, 0, 0))] * (slots * parts)
        + [pl.BlockSpec(mask.shape, lambda q: (0, 0))]
        + [pl.BlockSpec((1, cols, lanes), lambda q: (first + q, 0, 0))] * 2,
        out_specs=pl.BlockSpec((dests, all_rows, lanes), lambda q: (q, 0, 0)),
        out_shape=jax.ShapeDtypeStruct((number * dests, all_rows, lanes), BF16),
        compiler_params=pltpu.CompilerParams(vmem_limit_bytes=48 << 20),
        name="predict",
    )(*row_parts, *[x for part in spectra_parts for x in part], *consts)


def ring_of(length):
    return list(range(0, length, 2)) + list(range(1, length, 2))[::-1]


def shards(devices, members, traces, offset_bin, filters, data_matrix):
    shot_count, block, _ = traces.shape
    freqs, _, row_count, _ = data_matrix.shape
    lines = devices // members
    ring = ring_of(lines)
    after = {ring[i]: ring[(i + 1) % lines] for i in range(lines)}
    before = {b: a for a, b in after.items()}
    blocks = np.zeros((devices, members, lines), np.int32)
    for device in range(devices):
        line, member = divmod(device, members)
        for slot in range(lines):
            for m in range(members):
                blocks[device, m, slot] = line * members + (member ^ m)
            line = before[line]

    bands = freqs // BAND
    head = max(bands - 1, 1)
    first_parts, rest_parts = [None] * members, [None] * members

    def exchange(m):
        first, rest = rows_for(data_matrix, blocks[:, m], block, head)
        pairs = [(i, i ^ m) for i in range(devices)]
        if m:
            first = lax.ppermute(first, "rows", pairs)
            rest = lax.ppermute(rest, "rows", pairs)
        first_parts[m], rest_parts[m] = first, rest

    for m in range(members - 1, -1, -1):
        exchange(m)

    spectra_parts = [[x] for x in spectra_of(traces, offset_bin, filters, freqs)]
    step = [(i, after[i // members] * members + i % members) for i in range(devices)]
    for _ in range(lines - 1):
        for part in spectra_parts:
            part.append(lax.ppermute(part[-1], "rows", step))
    if block % 128:
        spectra_parts = [[jnp.concatenate(part, axis=1)] for part in spectra_parts]
        joined = lambda x: jnp.concatenate([x[:, i : i + 1] for i in range(lines)], axis=5)
        first_parts = [joined(x) for x in first_parts]
        rest_parts = [joined(x) for x in rest_parts]

    share = freqs // devices
    early = predict(first_parts, spectra_parts, share, 0)
    late = predict(rest_parts, spectra_parts, share, head)
    partial_value = jnp.concatenate([early, late], axis=0)
    received = lax.all_to_all(partial_value, "rows", split_axis=0, concat_axis=0, tiled=True)
    choose = np.zeros((lines, members, members, row_count, lines, members, row_count))
    for line in range(lines):
        for member in range(members):
            for j in range(members):
                for r in range(row_count):
                    choose[line, member, member ^ j, r, line, j, r] = 1.0
    rows = devices * members * row_count
    choose = jnp.asarray(choose.reshape(rows, devices * row_count), BF16)
    final = dot(received.reshape(rows, -1), choose, ((0,), (0,)))
    return final.astype(BF16).reshape(share, 2, shot_count, devices * row_count)


def solution(mesh):
    devices = mesh.shape["rows"]
    members = math.gcd(devices, 4)
    in_specs = (P("parts", "rows", None), P("parts", "rows"), P(), P("parts", None, "rows", None))
    out_specs = P(("parts", "rows"), None, None, None)
    return jax.shard_map(
        functools.partial(shards, devices, members),
        mesh=mesh,
        in_specs=in_specs,
        out_specs=out_specs,
        check_vma=False,
    )
```

```python
import functools
import math

import jax
import jax.numpy as jnp
import numpy as np
from jax import lax
from jax.experimental import pallas as pl
from jax.experimental.pallas import tpu as pltpu
from jax.sharding import PartitionSpec as P


FIRST = 64
BAND = 16
F32 = jnp.float32
BF16 = jnp.bfloat16


def dot(a, b, dims=((1,), (0,)), **kw):
    return lax.dot_general(a, b, (dims, ((), ())), preferred_element_type=F32, **kw)


def split(x, parts):
    pieces = []
    for _ in range(parts):
        piece = x.astype(BF16)
        pieces.append(piece)
        x = x - piece.astype(F32)
    return pieces


def transform_tables(freqs, length, taps):
    bands = freqs // BAND
    order = FIRST + np.arange(freqs).reshape(bands, 1, BAND)
    lanes = 2 * freqs

    def wave(samples, norm):
        angle = 2.0 * np.pi * ((samples[:, None, None, None] * order) % length) / length
        re, im = np.cos(angle) * norm, -np.sin(angle) * norm
        plain = np.concatenate([re, im], axis=2).reshape(len(samples), -1)
        swapped = np.concatenate([im, re], axis=2).reshape(len(samples), -1)
        return plain, swapped

    plain, swapped = wave(np.arange(length), 1.0 / math.sqrt(length))
    main = np.concatenate([plain, swapped], axis=1)
    main[length - taps :] = 0.0
    one, _ = wave(np.arange(taps), 1.0)
    one = one.reshape(taps, bands, 2, BAND)
    resp_a = np.concatenate([one[:, :, :1], one[:, :, :1]], axis=2).reshape(taps, -1)
    resp_b = np.concatenate([-one[:, :, 1:], one[:, :, 1:]], axis=2).reshape(taps, -1)
    resp = np.concatenate([resp_a, resp_b], axis=1)
    tail = np.zeros((lanes, lanes))
    tail[:taps] = plain[length - taps :]
    return jnp.asarray(main, BF16), jnp.asarray(resp, F32), jnp.asarray(tail, BF16)


def prepare(bins, taps, width, filt, resp, tail, select, last):
    filt_parts, resp_parts = split(filt[...], 2), split(resp[...], 2)
    table = dot(
        jnp.concatenate([filt_parts[0], filt_parts[1], filt_parts[0]], axis=1),
        jnp.concatenate([resp_parts[0], resp_parts[0], resp_parts[1]], axis=0),
    )
    select[...] = jnp.zeros_like(select)
    for i, piece in enumerate(split(table, 2)):
        select[i * bins : (i + 1) * bins, :] = piece
    rows = []
    for b in range(bins):
        row = jnp.pad(filt[b : b + 1, :], ((0, 0), (0, width - taps)))
        row = jnp.broadcast_to(row, (taps, width))
        rows.append(pltpu.roll(row, 0, 1, stride=1, stride_axis=0))
    rows = jnp.concatenate(rows, axis=0)
    high, low = split(rows, 2)
    last[...] = (dot(high, tail[...]) + dot(low, tail[...])).astype(BF16)


def chunk_of(shot, band, per):
    return shot // per * per + (band + shot % per) % per


def spectra_kernel(bands, bins, taps, part, outs, *refs):
    trace, bin_of, main_hbm = refs[:3]
    first = part == 0
    main, binned, sem = refs[-3:]
    if first:
        filt, resp, tail = refs[3:6]
        out_refs, (select, last) = refs[6 : 6 + outs], refs[6 + outs : 8 + outs]
    else:
        select, last = refs[3:5]
        out_refs = refs[5 : 5 + outs]
    places = [(ref, i) for ref in out_refs for i in range(ref.shape[0])]
    step = pl.program_id(0)
    width = main.shape[1] // 2
    count = bin_of.shape[1]
    shots = binned.shape[0]
    group, _, length = trace.shape
    copy = pltpu.make_async_copy(main_hbm, main, sem)

    @pl.when(step == 0)
    def _():
        copy.start()
        column = jnp.transpose(bin_of[...].astype(F32), (1, 0))
        for shot in range(shots):
            at = part * shots + shot
            value = jnp.broadcast_to(column[:, at : at + 1], (count, width))
            binned[shot] = value.astype(BF16)
        if first:
            prepare(bins, taps, width, filt, resp, tail, select, last)
        copy.wait()

    signal = trace[...].reshape(group * count, length)
    of = binned[pl.ds(step * group, group)].reshape(group * count, width).astype(F32)
    lane = lax.broadcasted_iota(jnp.int32, (1, width), 1)
    lane_bin = jnp.where(lane < 2 * bins, lane % bins, -1).astype(F32)
    chosen = jnp.where(of == lane_bin, 1.0, 0.0).astype(BF16)
    looked = dot(chosen, select[...])
    ends = signal[:, length - width :].astype(F32)
    shift = taps
    while shift < width:
        ends = jnp.where(lane >= width - shift, ends, pltpu.roll(ends, width - shift, 1))
        shift *= 2
    every = width // taps
    ending = [
        jnp.where(of == (lane // taps + base).astype(F32), ends, 0.0).astype(BF16)
        for base in range(0, bins, every)
    ]
    ending = jnp.concatenate(ending, axis=1)
    spectrum = dot(signal, main[...])
    value = (
        spectrum[:, :width] * looked[:, :width]
        + spectrum[:, width:] * looked[:, width:]
        + dot(ending, last[...])
    )
    chunk = 2 * BAND
    per = width // chunk
    place = lax.broadcasted_iota(jnp.int32, (count, width), 1) // chunk
    for phase in range(per // group):

        @pl.when(step == phase)
        def _():
            moved = []
            for i in range(group):
                j = phase * group + i
                part = value[i * count : (i + 1) * count]
                moved.append(part if j == 0 else pltpu.roll(part, j * chunk, 1))
            for band in range(bands):
                out, at = places[band]
                result = moved[0] if phase == 0 else out[at].astype(F32)
                for i in range(group):
                    j = phase * group + i
                    if j:
                        result = jnp.where(place == (band + j) % per, moved[i], result)
                out[at] = result.astype(BF16)


def spectra_of(traces, offset_bin, filters, freqs, cuts):
    shots, count, length = traces.shape
    bins, taps = filters.shape
    bands = freqs // BAND
    width = 2 * freqs
    group = 2
    main, resp, tail = transform_tables(freqs, length, taps)
    per = width // (2 * BAND)
    made = [
        jax.ShapeDtypeStruct((width, 2 * width), BF16),
        jax.ShapeDtypeStruct((taps * bins, width), BF16),
    ]
    whole = lambda x: pl.BlockSpec(x.shape, lambda s: (0,) * len(x.shape))
    results, extra = [], None
    for part in range(shots // per):
        first = part == 0
        more = [filters, resp, tail] if first else extra
        cut = cuts[part]
        shapes = [jax.ShapeDtypeStruct((b - a, count, width), BF16) for a, b in cut]
        outs = pl.pallas_call(
            functools.partial(spectra_kernel, bands, bins, taps, part, len(cut)),
            grid=(per // group,),
            in_specs=[
                pl.BlockSpec(
                    (group, count, length),
                    functools.partial(lambda p, s: (p + s, 0, 0), part * per // group),
                ),
                whole(offset_bin),
                pl.BlockSpec(memory_space=pltpu.HBM),
            ]
            + [whole(x) for x in more],
            out_specs=[whole(x) for x in shapes] + ([whole(x) for x in made] if first else []),
            out_shape=shapes + (made if first else []),
            scratch_shapes=[
                pltpu.VMEM(main.shape, BF16),
                pltpu.VMEM((per, count, width), BF16),
                pltpu.SemaphoreType.DMA,
            ],
            compiler_params=pltpu.CompilerParams(vmem_limit_bytes=60 << 20),
            cost_estimate=pl.CostEstimate(
                flops=2 * per * count * length * 2 * width,
                bytes_accessed=per * count * length * 2,
                transcendentals=0,
            ),
            name="spectra",
        )(traces, offset_bin, main, *more)
        if first:
            extra = outs[len(cut) :]
        results.append(outs[: len(cut)])
    return results


def rows_kernel(block, head, starts, source, first, rest, buffer, in_sems, out_sems):
    slots = buffer.shape[1]
    bands = buffer.shape[0]
    ins = []
    device = lax.axis_index("rows")
    for i in range(slots):
        start = jnp.int32(0)
        for d, row in enumerate(starts):
            start = jnp.where(device == d, jnp.int32(int(row[i]) * block), start)
        column = pl.multiple_of(start, block)
        ins.append(
            pltpu.make_async_copy(
                source.at[:, :, :, :, pl.ds(column, block)], buffer.at[:, i], in_sems.at[i]
            )
        )
        ins[-1].start()
    outs = []
    for i in range(slots):
        ins[i].wait()
        for k, (low, high, target) in enumerate(((0, head, first), (head, bands, rest))):
            copy = pltpu.make_async_copy(
                buffer.at[low:high, i], target.at[:, i], out_sems.at[i, k]
            )
            copy.start()
            outs.append(copy)
    for copy in outs:
        copy.wait()


def rows_for(data_matrix, starts, block, head):
    freqs, parts, rows, _ = data_matrix.shape
    bands = freqs // BAND
    slots = starts.shape[1]
    source = data_matrix.reshape(bands, BAND, parts, rows, -1)
    if block % 128:
        starts = jnp.asarray(starts)[lax.axis_index("rows")]
        pieces = [
            lax.dynamic_slice_in_dim(source, starts[i] * block, block, 4) for i in range(slots)
        ]
        both = jnp.stack(pieces, axis=1)
        return both[:head], both[head:]
    shape = (slots, BAND, parts, rows, block)
    kind = data_matrix.dtype
    return pl.pallas_call(
        functools.partial(rows_kernel, block, head, starts),
        in_specs=[pl.BlockSpec(memory_space=pltpu.HBM)],
        out_specs=[pl.BlockSpec(memory_space=pltpu.HBM)] * 2,
        out_shape=[
            jax.ShapeDtypeStruct((head,) + shape, kind),
            jax.ShapeDtypeStruct((bands - head,) + shape, kind),
        ],
        scratch_shapes=[
            pltpu.VMEM((bands,) + shape, kind),
            pltpu.SemaphoreType.DMA((slots,)),
            pltpu.SemaphoreType.DMA((slots, 2)),
        ],
        name="rows_for",
    )(source)


def merge_kernel(*refs):
    rows_in, out = refs[:-1], refs[-1]
    block = rows_in[0].shape[-1]
    for i in range(rows_in[0].shape[1]):
        part = jnp.concatenate([r[0, i] for r in rows_in], axis=2)
        out[0, :, i * block : (i + 1) * block] = part.reshape(-1, block)


def merge(row_parts):
    number, pieces, _, parts, rows, block = row_parts[0].shape
    shape = (BAND * parts * rows * len(row_parts), pieces * block)
    return pl.pallas_call(
        merge_kernel,
        grid=(number,),
        in_specs=[
            pl.BlockSpec((1, pieces, BAND, parts, rows, block), lambda q: (q, 0, 0, 0, 0, 0))
        ]
        * len(row_parts),
        out_specs=pl.BlockSpec((1,) + shape, lambda q: (q, 0, 0)),
        out_shape=jax.ShapeDtypeStruct((number,) + shape, row_parts[0].dtype),
        compiler_params=pltpu.CompilerParams(vmem_limit_bytes=40 << 20),
        name="merge",
    )(*row_parts)


def predict_kernel(parts, slots, before, matrix, *refs):
    spectra_in = refs[: slots * parts]
    mask_ref, fold_a, fold_b = refs[slots * parts : slots * parts + 3]
    out = refs[-1]
    spectra = [
        jnp.concatenate([spectra_in[p * slots + i][0] for p in range(parts)], axis=1)
        for i in range(slots)
    ]
    spectra = spectra[0] if slots == 1 else jnp.concatenate(spectra, axis=0)
    dests, rows, _ = out.shape
    total = dot(matrix[0], spectra)
    total = total.reshape(BAND, 2, rows, -1)
    acc = None
    for c, fold in enumerate((fold_a, fold_b)):
        value = total[:, c].reshape(BAND * rows, -1)
        value = jnp.where(mask_ref[...] != 0, value, 0.0)
        for piece in split(value, 2):
            term = dot(piece, fold[0])
            acc = term if acc is None else acc + term
    acc = acc.reshape(dests, BAND // dests, rows, -1)
    value = acc[:, 0]
    for i in range(1, BAND // dests):
        value = value + acc[:, i]
    if before:
        value = value + refs[-2][...].astype(F32)
    out[...] = value.astype(out.dtype)


def predict(matrix, spectra_parts, share, shots, first, part, before=None):
    number, wide, depth = matrix.shape
    parts, slots = len(spectra_parts), len(spectra_parts[0])
    _, block, width = spectra_parts[0][0].shape
    cols = width * parts
    per = width // (2 * BAND)
    all_rows = wide // (2 * BAND)
    lanes = share * 2 * shots
    index = np.arange(cols)
    col_c, col_f = index // BAND % 2, index % BAND
    row_f = np.arange(BAND * all_rows) // all_rows
    mask = (row_f[:, None] == col_f[None, :]).astype(np.float32)
    fold_a = np.zeros((number, cols, share, 2, shots), np.float32)
    fold_b = np.zeros((number, cols, share, 2, shots), np.float32)
    for band in range(number):
        shot_at = np.zeros(shots, np.int64)
        for shot in range(shots):
            shot_at[chunk_of(shot, first + band, per)] = shot
        col_s = shot_at[part * per + index // (2 * BAND)]
        fold_a[band, index, col_f % share, col_c, col_s] = 1.0
        fold_b[band, index, col_f % share, 1 - col_c, col_s] = np.where(col_c == 1, -1.0, 1.0)
    consts = [
        jnp.asarray(mask, F32),
        jnp.asarray(fold_a.reshape(number, cols, lanes), BF16),
        jnp.asarray(fold_b.reshape(number, cols, lanes), BF16),
    ]
    dests = BAND // share
    out_spec = pl.BlockSpec((dests, all_rows, lanes), lambda q: (q, 0, 0))
    flat = [x for spectra in spectra_parts for x in spectra]
    starts = [first * (x.shape[0] > number) for x in flat]
    return pl.pallas_call(
        functools.partial(predict_kernel, parts, slots, before is not None),
        grid=(number,),
        in_specs=[pl.BlockSpec((1, wide, depth), lambda q: (q, 0, 0))]
        + [
            pl.BlockSpec((1, block, width), functools.partial(lambda a, q: (a + q, 0, 0), a))
            for a in starts
        ]
        + [pl.BlockSpec(mask.shape, lambda q: (0, 0))]
        + [pl.BlockSpec((1, cols, lanes), lambda q: (q, 0, 0))] * 2
        + ([] if before is None else [out_spec]),
        out_specs=out_spec,
        out_shape=jax.ShapeDtypeStruct((number * dests, all_rows, lanes), BF16),
        compiler_params=pltpu.CompilerParams(vmem_limit_bytes=40 << 20),
        name="predict",
    )(matrix, *flat, *consts, *([] if before is None else [before]))


def ring_of(length):
    return list(range(0, length, 2)) + list(range(1, length, 2))[::-1]


def shards(devices, members, traces, offset_bin, filters, data_matrix):
    shot_count, block, _ = traces.shape
    freqs, _, row_count, _ = data_matrix.shape
    lines = devices // members
    ring = ring_of(lines)
    after = {ring[i]: ring[(i + 1) % lines] for i in range(lines)}
    before = {b: a for a, b in after.items()}
    blocks = np.zeros((devices, members, lines), np.int32)
    for device in range(devices):
        line, member = divmod(device, members)
        for slot in range(lines):
            for m in range(members):
                blocks[device, m, slot] = line * members + (member ^ m)
            line = before[line]

    bands = freqs // BAND
    head = max(bands - 1, 1)
    first_parts, rest_parts = [None] * members, [None] * members

    def exchange(m):
        first, rest = rows_for(data_matrix, blocks[:, m], block, head)
        pairs = [(i, i ^ m) for i in range(devices)]
        if m:
            first = lax.ppermute(first, "rows", pairs)
            rest = lax.ppermute(rest, "rows", pairs)
        first_parts[m], rest_parts[m] = first, rest

    for m in range(members - 1, -1, -1):
        exchange(m)

    per = 2 * freqs // (2 * BAND)
    quads = shot_count // per
    cuts = [[(0, bands)]] * (quads - 1) + [[(0, head), (head, bands)] if bands > head else [(0, bands)]]
    pieces = [(p, [x]) for p, cut in enumerate(spectra_of(traces, offset_bin, filters, freqs, cuts)) for x in cut]
    step = [(i, after[i // members] * members + i % members) for i in range(devices)]
    for _ in range(lines - 1):
        for _, piece in pieces:
            piece.append(lax.ppermute(piece[-1], "rows", step))
    if block % 128:
        pieces = [(p, [jnp.concatenate(piece, axis=1)]) for p, piece in pieces]
        joined = lambda x: jnp.concatenate([x[:, i : i + 1] for i in range(lines)], axis=5)
        first_parts = [joined(x) for x in first_parts]
        rest_parts = [joined(x) for x in rest_parts]

    share = freqs // devices
    first_matrix = merge(first_parts)
    rest_matrix = merge(rest_parts)
    whole_pieces = [piece for _, piece in pieces[: quads - 1]]
    head_piece, rest_piece = pieces[quads - 1][1], pieces[-1][1]
    early = predict(first_matrix, whole_pieces, share, shot_count, 0, 0)
    early = predict(first_matrix, [head_piece], share, shot_count, 0, quads - 1, early)
    late = predict(rest_matrix, whole_pieces + [rest_piece], share, shot_count, head, 0)
    partial_value = jnp.concatenate([early, late], axis=0)
    received = lax.all_to_all(partial_value, "rows", split_axis=0, concat_axis=0, tiled=True)
    choose = np.zeros((lines, members, members, row_count, lines, members, row_count))
    for line in range(lines):
        for member in range(members):
            for j in range(members):
                for r in range(row_count):
                    choose[line, member, member ^ j, r, line, j, r] = 1.0
    rows = devices * members * row_count
    choose = jnp.asarray(choose.reshape(rows, devices * row_count), BF16)
    final = dot(received.reshape(rows, -1), choose, ((0,), (0,)))
    return final.astype(BF16).reshape(share, 2, shot_count, devices * row_count)


def solution(mesh):
    devices = mesh.shape["rows"]
    members = math.gcd(devices, 4)
    in_specs = (P("parts", "rows", None), P("parts", "rows"), P(), P("parts", None, "rows", None))
    out_specs = P(("parts", "rows"), None, None, None)
    return jax.shard_map(
        functools.partial(shards, devices, members),
        mesh=mesh,
        in_specs=in_specs,
        out_specs=out_specs,
        check_vma=False,
    )
```

```python
import functools
import math

import jax
import jax.numpy as jnp
import numpy as np
from jax import lax
from jax.experimental import pallas as pl
from jax.experimental.pallas import tpu as pltpu
from jax.sharding import PartitionSpec as P


FIRST = 64
BAND = 16
F32 = jnp.float32
BF16 = jnp.bfloat16


def dot(a, b, dims=((1,), (0,)), **kw):
    return lax.dot_general(a, b, (dims, ((), ())), preferred_element_type=F32, **kw)


def split(x, parts):
    pieces = []
    for _ in range(parts):
        piece = x.astype(BF16)
        pieces.append(piece)
        x = x - piece.astype(F32)
    return pieces


def transform_tables(freqs, length, taps):
    bands = freqs // BAND
    order = FIRST + np.arange(freqs).reshape(bands, 1, BAND)
    lanes = 2 * freqs

    def wave(samples, norm):
        angle = 2.0 * np.pi * ((samples[:, None, None, None] * order) % length) / length
        re, im = np.cos(angle) * norm, -np.sin(angle) * norm
        plain = np.concatenate([re, im], axis=2).reshape(len(samples), -1)
        swapped = np.concatenate([im, re], axis=2).reshape(len(samples), -1)
        return plain, swapped

    plain, swapped = wave(np.arange(length), 1.0 / math.sqrt(length))
    main = np.concatenate([plain, swapped], axis=1)
    main[length - taps :] = 0.0
    one, _ = wave(np.arange(taps), 1.0)
    one = one.reshape(taps, bands, 2, BAND)
    resp_a = np.concatenate([one[:, :, :1], one[:, :, :1]], axis=2).reshape(taps, -1)
    resp_b = np.concatenate([-one[:, :, 1:], one[:, :, 1:]], axis=2).reshape(taps, -1)
    resp = np.concatenate([resp_a, resp_b], axis=1)
    tail = np.zeros((lanes, lanes))
    tail[:taps] = plain[length - taps :]
    return jnp.asarray(main, BF16), jnp.asarray(resp, F32), jnp.asarray(tail, BF16)


def prepare(bins, taps, width, filt, resp, tail, select, last):
    filt_parts, resp_parts = split(filt[...], 2), split(resp[...], 2)
    table = dot(
        jnp.concatenate([filt_parts[0], filt_parts[1], filt_parts[0]], axis=1),
        jnp.concatenate([resp_parts[0], resp_parts[0], resp_parts[1]], axis=0),
    )
    select[...] = jnp.zeros_like(select)
    for i, piece in enumerate(split(table, 2)):
        select[i * bins : (i + 1) * bins, :] = piece
    rows = []
    for b in range(bins):
        row = jnp.pad(filt[b : b + 1, :], ((0, 0), (0, width - taps)))
        row = jnp.broadcast_to(row, (taps, width))
        rows.append(pltpu.roll(row, 0, 1, stride=1, stride_axis=0))
    rows = jnp.concatenate(rows, axis=0)
    high, low = split(rows, 2)
    last[...] = (dot(high, tail[...]) + dot(low, tail[...])).astype(BF16)


def chunk_of(shot, band, per):
    return shot // per * per + (band + shot % per) % per


def spectra_kernel(bands, bins, taps, part, outs, *refs):
    trace, bin_of, main_hbm = refs[:3]
    first = part == 0
    main, binned, sem = refs[-3:]
    if first:
        filt, resp, tail = refs[3:6]
        out_refs, (select, last) = refs[6 : 6 + outs], refs[6 + outs : 8 + outs]
    else:
        select, last = refs[3:5]
        out_refs = refs[5 : 5 + outs]
    places = [(ref, i) for ref in out_refs for i in range(ref.shape[0])]
    step = pl.program_id(0)
    width = main.shape[1] // 2
    count = bin_of.shape[1]
    shots = binned.shape[0]
    group, _, length = trace.shape
    copy = pltpu.make_async_copy(main_hbm, main, sem)

    @pl.when(step == 0)
    def _():
        copy.start()
        column = jnp.transpose(bin_of[...].astype(F32), (1, 0))
        for shot in range(shots):
            at = part * shots + shot
            value = jnp.broadcast_to(column[:, at : at + 1], (count, width))
            binned[shot] = value.astype(BF16)
        if first:
            prepare(bins, taps, width, filt, resp, tail, select, last)
        copy.wait()

    signal = trace[...].reshape(group * count, length)
    of = binned[pl.ds(step * group, group)].reshape(group * count, width).astype(F32)
    lane = lax.broadcasted_iota(jnp.int32, (1, width), 1)
    lane_bin = jnp.where(lane < 2 * bins, lane % bins, -1).astype(F32)
    chosen = jnp.where(of == lane_bin, 1.0, 0.0).astype(BF16)
    looked = dot(chosen, select[...])
    ends = signal[:, length - width :].astype(F32)
    shift = taps
    while shift < width:
        ends = jnp.where(lane >= width - shift, ends, pltpu.roll(ends, width - shift, 1))
        shift *= 2
    every = width // taps
    ending = [
        jnp.where(of == (lane // taps + base).astype(F32), ends, 0.0).astype(BF16)
        for base in range(0, bins, every)
    ]
    ending = jnp.concatenate(ending, axis=1)
    spectrum = dot(signal, main[...])
    value = (
        spectrum[:, :width] * looked[:, :width]
        + spectrum[:, width:] * looked[:, width:]
        + dot(ending, last[...])
    )
    chunk = 2 * BAND
    per = width // chunk
    place = lax.broadcasted_iota(jnp.int32, (count, width), 1) // chunk
    for phase in range(per // group):

        @pl.when(step == phase)
        def _():
            moved = []
            for i in range(group):
                j = phase * group + i
                part = value[i * count : (i + 1) * count]
                moved.append(part if j == 0 else pltpu.roll(part, j * chunk, 1))
            for band in range(bands):
                out, at = places[band]
                result = moved[0] if phase == 0 else out[at].astype(F32)
                for i in range(group):
                    j = phase * group + i
                    if j:
                        result = jnp.where(place == (band + j) % per, moved[i], result)
                out[at] = result.astype(BF16)


def spectra_of(traces, offset_bin, filters, freqs, cuts):
    shots, count, length = traces.shape
    bins, taps = filters.shape
    bands = freqs // BAND
    width = 2 * freqs
    group = 2
    main, resp, tail = transform_tables(freqs, length, taps)
    per = width // (2 * BAND)
    made = [
        jax.ShapeDtypeStruct((width, 2 * width), BF16),
        jax.ShapeDtypeStruct((taps * bins, width), BF16),
    ]
    whole = lambda x: pl.BlockSpec(x.shape, lambda s: (0,) * len(x.shape))
    results, extra = [], None
    for part in range(shots // per):
        first = part == 0
        more = [filters, resp, tail] if first else extra
        cut = cuts[part]
        shapes = [jax.ShapeDtypeStruct((b - a, count, width), BF16) for a, b in cut]
        outs = pl.pallas_call(
            functools.partial(spectra_kernel, bands, bins, taps, part, len(cut)),
            grid=(per // group,),
            in_specs=[
                pl.BlockSpec(
                    (group, count, length),
                    functools.partial(lambda p, s: (p + s, 0, 0), part * per // group),
                ),
                whole(offset_bin),
                pl.BlockSpec(memory_space=pltpu.HBM),
            ]
            + [whole(x) for x in more],
            out_specs=[whole(x) for x in shapes] + ([whole(x) for x in made] if first else []),
            out_shape=shapes + (made if first else []),
            scratch_shapes=[
                pltpu.VMEM(main.shape, BF16),
                pltpu.VMEM((per, count, width), BF16),
                pltpu.SemaphoreType.DMA,
            ],
            compiler_params=pltpu.CompilerParams(vmem_limit_bytes=60 << 20),
            cost_estimate=pl.CostEstimate(
                flops=2 * per * count * length * 2 * width,
                bytes_accessed=per * count * length * 2,
                transcendentals=0,
            ),
            name="spectra",
        )(traces, offset_bin, main, *more)
        if first:
            extra = outs[len(cut) :]
        results.append(outs[: len(cut)])
    return results


def rows_kernel(block, head, starts, source, first, rest, buffer, in_sems, out_sems):
    slots = buffer.shape[1]
    bands = buffer.shape[0]
    ins = []
    device = lax.axis_index("rows")
    for i in range(slots):
        start = jnp.int32(0)
        for d, row in enumerate(starts):
            start = jnp.where(device == d, jnp.int32(int(row[i]) * block), start)
        column = pl.multiple_of(start, block)
        ins.append(
            pltpu.make_async_copy(
                source.at[:, :, :, :, pl.ds(column, block)], buffer.at[:, i], in_sems.at[i]
            )
        )
        ins[-1].start()
    outs = []
    for i in range(slots):
        ins[i].wait()
        for k, (low, high, target) in enumerate(((0, head, first), (head, bands, rest))):
            copy = pltpu.make_async_copy(
                buffer.at[low:high, i], target.at[:, i], out_sems.at[i, k]
            )
            copy.start()
            outs.append(copy)
    for copy in outs:
        copy.wait()


def rows_for(data_matrix, starts, block, head):
    freqs, parts, rows, _ = data_matrix.shape
    bands = freqs // BAND
    slots = starts.shape[1]
    source = data_matrix.reshape(bands, BAND, parts, rows, -1)
    if block % 128:
        starts = jnp.asarray(starts)[lax.axis_index("rows")]
        pieces = [
            lax.dynamic_slice_in_dim(source, starts[i] * block, block, 4) for i in range(slots)
        ]
        both = jnp.stack(pieces, axis=1)
        return both[:head], both[head:]
    shape = (slots, BAND, parts, rows, block)
    kind = data_matrix.dtype
    return pl.pallas_call(
        functools.partial(rows_kernel, block, head, starts),
        in_specs=[pl.BlockSpec(memory_space=pltpu.HBM)],
        out_specs=[pl.BlockSpec(memory_space=pltpu.HBM)] * 2,
        out_shape=[
            jax.ShapeDtypeStruct((head,) + shape, kind),
            jax.ShapeDtypeStruct((bands - head,) + shape, kind),
        ],
        scratch_shapes=[
            pltpu.VMEM((bands,) + shape, kind),
            pltpu.SemaphoreType.DMA((slots,)),
            pltpu.SemaphoreType.DMA((slots, 2)),
        ],
        name="rows_for",
    )(source)


def merged(rows_in):
    columns = []
    for i in range(rows_in[0].shape[1]):
        part = jnp.concatenate([r[0, i] for r in rows_in], axis=2)
        columns.append(part.reshape(-1, part.shape[-1]))
    return columns


def merge_kernel(*refs):
    rows_in, out = refs[:-1], refs[-1]
    block = rows_in[0].shape[-1]
    for i, column in enumerate(merged(rows_in)):
        out[0, :, i * block : (i + 1) * block] = column


def merge(row_parts):
    number, pieces, _, parts, rows, block = row_parts[0].shape
    shape = (BAND * parts * rows * len(row_parts), pieces * block)
    return pl.pallas_call(
        merge_kernel,
        grid=(number,),
        in_specs=[
            pl.BlockSpec((1, pieces, BAND, parts, rows, block), lambda q: (q, 0, 0, 0, 0, 0))
        ]
        * len(row_parts),
        out_specs=pl.BlockSpec((1,) + shape, lambda q: (q, 0, 0)),
        out_shape=jax.ShapeDtypeStruct((number,) + shape, row_parts[0].dtype),
        compiler_params=pltpu.CompilerParams(vmem_limit_bytes=40 << 20),
        name="merge",
    )(*row_parts)


def predict_kernel(members, parts, slots, before, *refs):
    rows_in, refs = refs[:members], refs[members:]
    if members == 1:
        matrix = rows_in[0][0]
    else:
        columns = merged(rows_in)
        matrix = columns[0] if len(columns) == 1 else jnp.concatenate(columns, axis=1)
    spectra_in = refs[: slots * parts]
    mask_ref, fold_a, fold_b = refs[slots * parts : slots * parts + 3]
    out = refs[-1]
    spectra = [
        jnp.concatenate([spectra_in[p * slots + i][0] for p in range(parts)], axis=1)
        for i in range(slots)
    ]
    spectra = spectra[0] if slots == 1 else jnp.concatenate(spectra, axis=0)
    dests, rows, _ = out.shape
    total = dot(matrix, spectra)
    total = total.reshape(BAND, 2, rows, -1)
    acc = None
    for c, fold in enumerate((fold_a, fold_b)):
        value = total[:, c].reshape(BAND * rows, -1)
        value = jnp.where(mask_ref[...] != 0, value, 0.0)
        for piece in split(value, 2):
            term = dot(piece, fold[0])
            acc = term if acc is None else acc + term
    acc = acc.reshape(dests, BAND // dests, rows, -1)
    value = acc[:, 0]
    for i in range(1, BAND // dests):
        value = value + acc[:, i]
    if before:
        value = value + refs[-2][...].astype(F32)
    out[...] = value.astype(out.dtype)


def predict(matrix, spectra_parts, share, shots, first, part, before=None):
    if isinstance(matrix, list):
        number, _, _, _, rows, depth = matrix[0].shape
        all_rows = rows * len(matrix)
    else:
        number, wide, depth = matrix.shape
        all_rows = wide // (2 * BAND)
        matrix = [matrix]
    parts, slots = len(spectra_parts), len(spectra_parts[0])
    _, block, width = spectra_parts[0][0].shape
    cols = width * parts
    per = width // (2 * BAND)
    lanes = share * 2 * shots
    index = np.arange(cols)
    col_c, col_f = index // BAND % 2, index % BAND
    row_f = np.arange(BAND * all_rows) // all_rows
    mask = (row_f[:, None] == col_f[None, :]).astype(np.float32)
    fold_a = np.zeros((number, cols, share, 2, shots), np.float32)
    fold_b = np.zeros((number, cols, share, 2, shots), np.float32)
    for band in range(number):
        shot_at = np.zeros(shots, np.int64)
        for shot in range(shots):
            shot_at[chunk_of(shot, first + band, per)] = shot
        col_s = shot_at[part * per + index // (2 * BAND)]
        fold_a[band, index, col_f % share, col_c, col_s] = 1.0
        fold_b[band, index, col_f % share, 1 - col_c, col_s] = np.where(col_c == 1, -1.0, 1.0)
    consts = [
        jnp.asarray(mask, F32),
        jnp.asarray(fold_a.reshape(number, cols, lanes), BF16),
        jnp.asarray(fold_b.reshape(number, cols, lanes), BF16),
    ]
    dests = BAND // share
    out_spec = pl.BlockSpec((dests, all_rows, lanes), lambda q: (q, 0, 0))
    flat = [x for spectra in spectra_parts for x in spectra]
    starts = [first * (x.shape[0] > number) for x in flat]
    return pl.pallas_call(
        functools.partial(predict_kernel, len(matrix), parts, slots, before is not None),
        grid=(number,),
        in_specs=[
            pl.BlockSpec(
                (1,) + x.shape[1:], functools.partial(lambda n, q: (q,) + (0,) * n, x.ndim - 1)
            )
            for x in matrix
        ]
        + [
            pl.BlockSpec((1, block, width), functools.partial(lambda a, q: (a + q, 0, 0), a))
            for a in starts
        ]
        + [pl.BlockSpec(mask.shape, lambda q: (0, 0))]
        + [pl.BlockSpec((1, cols, lanes), lambda q: (q, 0, 0))] * 2
        + ([] if before is None else [out_spec]),
        out_specs=out_spec,
        out_shape=jax.ShapeDtypeStruct((number * dests, all_rows, lanes), BF16),
        compiler_params=pltpu.CompilerParams(vmem_limit_bytes=40 << 20),
        name="predict",
    )(*matrix, *flat, *consts, *([] if before is None else [before]))


def ring_of(length):
    return list(range(0, length, 2)) + list(range(1, length, 2))[::-1]


def shards(devices, members, traces, offset_bin, filters, data_matrix):
    shot_count, block, _ = traces.shape
    freqs, _, row_count, _ = data_matrix.shape
    lines = devices // members
    ring = ring_of(lines)
    after = {ring[i]: ring[(i + 1) % lines] for i in range(lines)}
    before = {b: a for a, b in after.items()}
    blocks = np.zeros((devices, members, lines), np.int32)
    for device in range(devices):
        line, member = divmod(device, members)
        for slot in range(lines):
            for m in range(members):
                blocks[device, m, slot] = line * members + (member ^ m)
            line = before[line]

    bands = freqs // BAND
    head = max(bands - 1, 1)
    first_parts, rest_parts = [None] * members, [None] * members

    def exchange(m):
        first, rest = rows_for(data_matrix, blocks[:, m], block, head)
        pairs = [(i, i ^ m) for i in range(devices)]
        if m:
            first = lax.ppermute(first, "rows", pairs)
            rest = lax.ppermute(rest, "rows", pairs)
        first_parts[m], rest_parts[m] = first, rest

    for m in range(members - 1, -1, -1):
        exchange(m)

    per = 2 * freqs // (2 * BAND)
    quads = shot_count // per
    cuts = [[(0, bands)]] * (quads - 1) + [[(0, head), (head, bands)] if bands > head else [(0, bands)]]
    pieces = [(p, [x]) for p, cut in enumerate(spectra_of(traces, offset_bin, filters, freqs, cuts)) for x in cut]
    step = [(i, after[i // members] * members + i % members) for i in range(devices)]
    for _ in range(lines - 1):
        for _, piece in pieces:
            piece.append(lax.ppermute(piece[-1], "rows", step))
    if block % 128:
        pieces = [(p, [jnp.concatenate(piece, axis=1)]) for p, piece in pieces]
        joined = lambda x: jnp.concatenate([x[:, i : i + 1] for i in range(lines)], axis=5)
        first_parts = [joined(x) for x in first_parts]
        rest_parts = [joined(x) for x in rest_parts]

    share = freqs // devices
    first_matrix = merge(first_parts)
    whole_pieces = [piece for _, piece in pieces[: quads - 1]]
    head_piece, rest_piece = pieces[quads - 1][1], pieces[-1][1]
    early = predict(first_matrix, whole_pieces, share, shot_count, 0, 0)
    early = predict(first_matrix, [head_piece], share, shot_count, 0, quads - 1, early)
    late = predict(rest_parts, whole_pieces + [rest_piece], share, shot_count, head, 0)
    partial_value = jnp.concatenate([early, late], axis=0)
    received = lax.all_to_all(partial_value, "rows", split_axis=0, concat_axis=0, tiled=True)
    choose = np.zeros((lines, members, members, row_count, lines, members, row_count))
    for line in range(lines):
        for member in range(members):
            for j in range(members):
                for r in range(row_count):
                    choose[line, member, member ^ j, r, line, j, r] = 1.0
    rows = devices * members * row_count
    choose = jnp.asarray(choose.reshape(rows, devices * row_count), BF16)
    final = dot(received.reshape(rows, -1), choose, ((0,), (0,)))
    return final.astype(BF16).reshape(share, 2, shot_count, devices * row_count)


def solution(mesh):
    devices = mesh.shape["rows"]
    members = math.gcd(devices, 4)
    in_specs = (P("parts", "rows", None), P("parts", "rows"), P(), P("parts", None, "rows", None))
    out_specs = P(("parts", "rows"), None, None, None)
    return jax.shard_map(
        functools.partial(shards, devices, members),
        mesh=mesh,
        in_specs=in_specs,
        out_specs=out_specs,
        check_vma=False,
    )
```

```python
import functools
import math

import jax
import jax.numpy as jnp
import numpy as np
from jax import lax
from jax.experimental import pallas as pl
from jax.experimental.pallas import tpu as pltpu
from jax.sharding import PartitionSpec as P


FIRST = 64
BAND = 16
F32 = jnp.float32
BF16 = jnp.bfloat16


def dot(a, b, dims=((1,), (0,)), **kw):
    return lax.dot_general(a, b, (dims, ((), ())), preferred_element_type=F32, **kw)


def split(x, parts):
    pieces = []
    for _ in range(parts):
        piece = x.astype(BF16)
        pieces.append(piece)
        x = x - piece.astype(F32)
    return pieces


def transform_tables(freqs, length, taps):
    bands = freqs // BAND
    order = FIRST + np.arange(freqs).reshape(bands, 1, BAND)
    lanes = 2 * freqs

    def wave(samples, norm):
        angle = 2.0 * np.pi * ((samples[:, None, None, None] * order) % length) / length
        re, im = np.cos(angle) * norm, -np.sin(angle) * norm
        plain = np.concatenate([re, im], axis=2).reshape(len(samples), -1)
        swapped = np.concatenate([im, re], axis=2).reshape(len(samples), -1)
        return plain, swapped

    plain, swapped = wave(np.arange(length), 1.0 / math.sqrt(length))
    main = np.concatenate([plain, swapped], axis=1)
    main[length - taps :] = 0.0
    one, _ = wave(np.arange(taps), 1.0)
    one = one.reshape(taps, bands, 2, BAND)
    resp_a = np.concatenate([one[:, :, :1], one[:, :, :1]], axis=2).reshape(taps, -1)
    resp_b = np.concatenate([-one[:, :, 1:], one[:, :, 1:]], axis=2).reshape(taps, -1)
    resp = np.concatenate([resp_a, resp_b], axis=1)
    tail = np.zeros((lanes, lanes))
    tail[:taps] = plain[length - taps :]
    return jnp.asarray(main, BF16), jnp.asarray(resp, F32), jnp.asarray(tail, BF16)


def prepare(bins, taps, width, filt, resp, tail, select, last):
    filt_parts, resp_parts = split(filt[...], 2), split(resp[...], 2)
    table = dot(
        jnp.concatenate([filt_parts[0], filt_parts[1], filt_parts[0]], axis=1),
        jnp.concatenate([resp_parts[0], resp_parts[0], resp_parts[1]], axis=0),
    )
    select[...] = jnp.zeros_like(select)
    for i, piece in enumerate(split(table, 2)):
        select[i * bins : (i + 1) * bins, :] = piece
    rows = []
    for b in range(bins):
        row = jnp.pad(filt[b : b + 1, :], ((0, 0), (0, width - taps)))
        row = jnp.broadcast_to(row, (taps, width))
        rows.append(pltpu.roll(row, 0, 1, stride=1, stride_axis=0))
    rows = jnp.concatenate(rows, axis=0)
    high, low = split(rows, 2)
    last[...] = (dot(high, tail[...]) + dot(low, tail[...])).astype(BF16)


def chunk_of(shot, band, per):
    return shot // per * per + (band + shot % per) % per


def spectra_kernel(bands, bins, taps, part, outs, *refs):
    trace, bin_of, main_hbm = refs[:3]
    first = part == 0
    main, binned, sem = refs[-3:]
    if first:
        filt, resp, tail = refs[3:6]
        out_refs, (select, last) = refs[6 : 6 + outs], refs[6 + outs : 8 + outs]
    else:
        select, last = refs[3:5]
        out_refs = refs[5 : 5 + outs]
    places = [(ref, i) for ref in out_refs for i in range(ref.shape[0])]
    step = pl.program_id(0)
    width = main.shape[1] // 2
    count = bin_of.shape[1]
    shots = binned.shape[0]
    group, _, length = trace.shape
    copy = pltpu.make_async_copy(main_hbm, main, sem)

    @pl.when(step == 0)
    def _():
        copy.start()
        column = jnp.transpose(bin_of[...].astype(F32), (1, 0))
        for shot in range(shots):
            at = part * shots + shot
            value = jnp.broadcast_to(column[:, at : at + 1], (count, width))
            binned[shot] = value.astype(BF16)
        if first:
            prepare(bins, taps, width, filt, resp, tail, select, last)
        copy.wait()

    signal = trace[...].reshape(group * count, length)
    of = binned[pl.ds(step * group, group)].reshape(group * count, width).astype(F32)
    lane = lax.broadcasted_iota(jnp.int32, (1, width), 1)
    lane_bin = jnp.where(lane < 2 * bins, lane % bins, -1).astype(F32)
    chosen = jnp.where(of == lane_bin, 1.0, 0.0).astype(BF16)
    looked = dot(chosen, select[...])
    ends = signal[:, length - width :].astype(F32)
    shift = taps
    while shift < width:
        ends = jnp.where(lane >= width - shift, ends, pltpu.roll(ends, width - shift, 1))
        shift *= 2
    every = width // taps
    ending = [
        jnp.where(of == (lane // taps + base).astype(F32), ends, 0.0).astype(BF16)
        for base in range(0, bins, every)
    ]
    ending = jnp.concatenate(ending, axis=1)
    spectrum = dot(signal, main[...])
    value = (
        spectrum[:, :width] * looked[:, :width]
        + spectrum[:, width:] * looked[:, width:]
        + dot(ending, last[...])
    )
    chunk = 2 * BAND
    per = width // chunk
    place = lax.broadcasted_iota(jnp.int32, (count, width), 1) // chunk
    for phase in range(per // group):

        @pl.when(step == phase)
        def _():
            moved = []
            for i in range(group):
                j = phase * group + i
                part = value[i * count : (i + 1) * count]
                moved.append(part if j == 0 else pltpu.roll(part, j * chunk, 1))
            for band in range(bands):
                out, at = places[band]
                result = moved[0] if phase == 0 else out[at].astype(F32)
                for i in range(group):
                    j = phase * group + i
                    if j:
                        result = jnp.where(place == (band + j) % per, moved[i], result)
                out[at] = result.astype(BF16)


def spectra_of(traces, offset_bin, filters, freqs, cuts):
    shots, count, length = traces.shape
    bins, taps = filters.shape
    bands = freqs // BAND
    width = 2 * freqs
    group = 2
    main, resp, tail = transform_tables(freqs, length, taps)
    per = width // (2 * BAND)
    made = [
        jax.ShapeDtypeStruct((width, 2 * width), BF16),
        jax.ShapeDtypeStruct((taps * bins, width), BF16),
    ]
    whole = lambda x: pl.BlockSpec(x.shape, lambda s: (0,) * len(x.shape))
    results, extra = [], None
    for part in range(shots // per):
        first = part == 0
        more = [filters, resp, tail] if first else extra
        cut = cuts[part]
        shapes = [jax.ShapeDtypeStruct((b - a, count, width), BF16) for a, b in cut]
        outs = pl.pallas_call(
            functools.partial(spectra_kernel, bands, bins, taps, part, len(cut)),
            grid=(per // group,),
            in_specs=[
                pl.BlockSpec(
                    (group, count, length),
                    functools.partial(lambda p, s: (p + s, 0, 0), part * per // group),
                ),
                whole(offset_bin),
                pl.BlockSpec(memory_space=pltpu.HBM),
            ]
            + [whole(x) for x in more],
            out_specs=[whole(x) for x in shapes] + ([whole(x) for x in made] if first else []),
            out_shape=shapes + (made if first else []),
            scratch_shapes=[
                pltpu.VMEM(main.shape, BF16),
                pltpu.VMEM((per, count, width), BF16),
                pltpu.SemaphoreType.DMA,
            ],
            compiler_params=pltpu.CompilerParams(vmem_limit_bytes=60 << 20),
            cost_estimate=pl.CostEstimate(
                flops=2 * per * count * length * 2 * width,
                bytes_accessed=per * count * length * 2,
                transcendentals=0,
            ),
            name="spectra",
        )(traces, offset_bin, main, *more)
        if first:
            extra = outs[len(cut) :]
        results.append(outs[: len(cut)])
    return results


def rows_kernel(block, head, starts, source, first, rest, buffer, in_sems, out_sems):
    slots = buffer.shape[1]
    bands = buffer.shape[0]
    ins = []
    device = lax.axis_index("rows")
    for i in range(slots):
        start = jnp.int32(0)
        for d, row in enumerate(starts):
            start = jnp.where(device == d, jnp.int32(int(row[i]) * block), start)
        column = pl.multiple_of(start, block)
        ins.append(
            pltpu.make_async_copy(
                source.at[:, :, :, :, pl.ds(column, block)], buffer.at[:, i], in_sems.at[i]
            )
        )
        ins[-1].start()
    outs = []
    for i in range(slots):
        ins[i].wait()
        for k, (low, high, target) in enumerate(((0, head, first), (head, bands, rest))):
            copy = pltpu.make_async_copy(
                buffer.at[low:high, i], target.at[:, i], out_sems.at[i, k]
            )
            copy.start()
            outs.append(copy)
    for copy in outs:
        copy.wait()


def rows_for(data_matrix, starts, block, head, limit=None):
    freqs, parts, rows, _ = data_matrix.shape
    bands = freqs // BAND
    slots = starts.shape[1]
    source = data_matrix.reshape(bands, BAND, parts, rows, -1)
    if block % 128:
        starts = jnp.asarray(starts)[lax.axis_index("rows")]
        pieces = [
            lax.dynamic_slice_in_dim(source, starts[i] * block, block, 4) for i in range(slots)
        ]
        both = jnp.stack(pieces, axis=1)
        return both[:head], both[head:]
    shape = (slots, BAND, parts, rows, block)
    kind = data_matrix.dtype
    return pl.pallas_call(
        functools.partial(rows_kernel, block, head, starts),
        in_specs=[pl.BlockSpec(memory_space=pltpu.HBM)],
        out_specs=[pl.BlockSpec(memory_space=pltpu.HBM)] * 2,
        out_shape=[
            jax.ShapeDtypeStruct((head,) + shape, kind),
            jax.ShapeDtypeStruct((bands - head,) + shape, kind),
        ],
        scratch_shapes=[
            pltpu.VMEM((bands,) + shape, kind),
            pltpu.SemaphoreType.DMA((slots,)),
            pltpu.SemaphoreType.DMA((slots, 2)),
        ],
        compiler_params=pltpu.CompilerParams(vmem_limit_bytes=limit),
        name="rows_for",
    )(source)


def merged(rows_in):
    columns = []
    for i in range(rows_in[0].shape[1]):
        part = jnp.concatenate([r[0, i] for r in rows_in], axis=2)
        columns.append(part.reshape(-1, part.shape[-1]))
    return columns


def merge_kernel(*refs):
    rows_in, out = refs[:-1], refs[-1]
    block = rows_in[0].shape[-1]
    for i, column in enumerate(merged(rows_in)):
        out[0, :, i * block : (i + 1) * block] = column


def merge(row_parts):
    number, pieces, _, parts, rows, block = row_parts[0].shape
    shape = (BAND * parts * rows * len(row_parts), pieces * block)
    return pl.pallas_call(
        merge_kernel,
        grid=(number,),
        in_specs=[
            pl.BlockSpec((1, pieces, BAND, parts, rows, block), lambda q: (q, 0, 0, 0, 0, 0))
        ]
        * len(row_parts),
        out_specs=pl.BlockSpec((1,) + shape, lambda q: (q, 0, 0)),
        out_shape=jax.ShapeDtypeStruct((number,) + shape, row_parts[0].dtype),
        compiler_params=pltpu.CompilerParams(vmem_limit_bytes=40 << 20),
        name="merge",
    )(*row_parts)


def predict_kernel(members, parts, slots, before, *refs):
    rows_in, refs = refs[:members], refs[members:]
    if members == 1:
        matrix = rows_in[0][0]
    else:
        columns = merged(rows_in)
        matrix = columns[0] if len(columns) == 1 else jnp.concatenate(columns, axis=1)
    spectra_in = refs[: slots * parts]
    mask_ref, fold_a, fold_b = refs[slots * parts : slots * parts + 3]
    out = refs[-1]
    spectra = [
        jnp.concatenate([spectra_in[p * slots + i][0] for p in range(parts)], axis=1)
        for i in range(slots)
    ]
    spectra = spectra[0] if slots == 1 else jnp.concatenate(spectra, axis=0)
    dests, rows, _ = out.shape
    total = dot(matrix, spectra)
    total = total.reshape(BAND, 2, rows, -1)
    acc = None
    for c, fold in enumerate((fold_a, fold_b)):
        value = total[:, c].reshape(BAND * rows, -1)
        value = jnp.where(mask_ref[...] != 0, value, 0.0)
        for piece in split(value, 2):
            term = dot(piece, fold[0])
            acc = term if acc is None else acc + term
    acc = acc.reshape(dests, BAND // dests, rows, -1)
    value = acc[:, 0]
    for i in range(1, BAND // dests):
        value = value + acc[:, i]
    if before:
        value = value + refs[-2][...].astype(F32)
    out[...] = value.astype(out.dtype)


def predict(matrix, spectra_parts, share, shots, first, part, before=None):
    if isinstance(matrix, list):
        number, _, _, _, rows, depth = matrix[0].shape
        all_rows = rows * len(matrix)
    else:
        number, wide, depth = matrix.shape
        all_rows = wide // (2 * BAND)
        matrix = [matrix]
    parts, slots = len(spectra_parts), len(spectra_parts[0])
    _, block, width = spectra_parts[0][0].shape
    cols = width * parts
    per = width // (2 * BAND)
    lanes = share * 2 * shots
    index = np.arange(cols)
    col_c, col_f = index // BAND % 2, index % BAND
    row_f = np.arange(BAND * all_rows) // all_rows
    mask = (row_f[:, None] == col_f[None, :]).astype(np.float32)
    fold_a = np.zeros((number, cols, share, 2, shots), np.float32)
    fold_b = np.zeros((number, cols, share, 2, shots), np.float32)
    for band in range(number):
        shot_at = np.zeros(shots, np.int64)
        for shot in range(shots):
            shot_at[chunk_of(shot, first + band, per)] = shot
        col_s = shot_at[part * per + index // (2 * BAND)]
        fold_a[band, index, col_f % share, col_c, col_s] = 1.0
        fold_b[band, index, col_f % share, 1 - col_c, col_s] = np.where(col_c == 1, -1.0, 1.0)
    consts = [
        jnp.asarray(mask, F32),
        jnp.asarray(fold_a.reshape(number, cols, lanes), BF16),
        jnp.asarray(fold_b.reshape(number, cols, lanes), BF16),
    ]
    dests = BAND // share
    out_spec = pl.BlockSpec((dests, all_rows, lanes), lambda q: (q, 0, 0))
    flat = [x for spectra in spectra_parts for x in spectra]
    starts = [first * (x.shape[0] > number) for x in flat]
    return pl.pallas_call(
        functools.partial(predict_kernel, len(matrix), parts, slots, before is not None),
        grid=(number,),
        in_specs=[
            pl.BlockSpec(
                (1,) + x.shape[1:], functools.partial(lambda n, q: (q,) + (0,) * n, x.ndim - 1)
            )
            for x in matrix
        ]
        + [
            pl.BlockSpec((1, block, width), functools.partial(lambda a, q: (a + q, 0, 0), a))
            for a in starts
        ]
        + [pl.BlockSpec(mask.shape, lambda q: (0, 0))]
        + [pl.BlockSpec((1, cols, lanes), lambda q: (q, 0, 0))] * 2
        + ([] if before is None else [out_spec]),
        out_specs=out_spec,
        out_shape=jax.ShapeDtypeStruct((number * dests, all_rows, lanes), BF16),
        compiler_params=pltpu.CompilerParams(vmem_limit_bytes=40 << 20),
        name="predict",
    )(*matrix, *flat, *consts, *([] if before is None else [before]))


def ring_of(length):
    return list(range(0, length, 2)) + list(range(1, length, 2))[::-1]


def shards(devices, members, traces, offset_bin, filters, data_matrix):
    shot_count, block, _ = traces.shape
    freqs, _, row_count, _ = data_matrix.shape
    lines = devices // members
    ring = ring_of(lines)
    after = {ring[i]: ring[(i + 1) % lines] for i in range(lines)}
    before = {b: a for a, b in after.items()}
    blocks = np.zeros((devices, members, lines), np.int32)
    for device in range(devices):
        line, member = divmod(device, members)
        for slot in range(lines):
            for m in range(members):
                blocks[device, m, slot] = line * members + (member ^ m)
            line = before[line]

    bands = freqs // BAND
    head = max(bands - 1, 1)
    first_parts, rest_parts = [None] * members, [None] * members

    def exchange(m):
        first, rest = rows_for(data_matrix, blocks[:, m], block, head, (40 << 20) if m < 2 else None)
        pairs = [(i, i ^ m) for i in range(devices)]
        if m:
            first = lax.ppermute(first, "rows", pairs)
            rest = lax.ppermute(rest, "rows", pairs)
        first_parts[m], rest_parts[m] = first, rest

    for m in range(members - 1, -1, -1):
        exchange(m)

    per = 2 * freqs // (2 * BAND)
    quads = shot_count // per
    cuts = [[(0, bands)]] * (quads - 1) + [[(0, head), (head, bands)] if bands > head else [(0, bands)]]
    pieces = [(p, [x]) for p, cut in enumerate(spectra_of(traces, offset_bin, filters, freqs, cuts)) for x in cut]
    step = [(i, after[i // members] * members + i % members) for i in range(devices)]
    for _ in range(lines - 1):
        for _, piece in pieces:
            piece.append(lax.ppermute(piece[-1], "rows", step))
    if block % 128:
        pieces = [(p, [jnp.concatenate(piece, axis=1)]) for p, piece in pieces]
        joined = lambda x: jnp.concatenate([x[:, i : i + 1] for i in range(lines)], axis=5)
        first_parts = [joined(x) for x in first_parts]
        rest_parts = [joined(x) for x in rest_parts]

    share = freqs // devices
    first_matrix = merge(first_parts)
    whole_pieces = [piece for _, piece in pieces[: quads - 1]]
    head_piece, rest_piece = pieces[quads - 1][1], pieces[-1][1]
    early = predict(first_matrix, whole_pieces, share, shot_count, 0, 0)
    early = predict(first_matrix, [head_piece], share, shot_count, 0, quads - 1, early)
    late = predict(rest_parts, whole_pieces + [rest_piece], share, shot_count, head, 0)
    partial_value = jnp.concatenate([early, late], axis=0)
    received = lax.all_to_all(partial_value, "rows", split_axis=0, concat_axis=0, tiled=True)
    choose = np.zeros((lines, members, members, row_count, lines, members, row_count))
    for line in range(lines):
        for member in range(members):
            for j in range(members):
                for r in range(row_count):
                    choose[line, member, member ^ j, r, line, j, r] = 1.0
    rows = devices * members * row_count
    choose = jnp.asarray(choose.reshape(rows, devices * row_count), BF16)
    final = dot(received.reshape(rows, -1), choose, ((0,), (0,)))
    return final.astype(BF16).reshape(share, 2, shot_count, devices * row_count)


def solution(mesh):
    devices = mesh.shape["rows"]
    members = math.gcd(devices, 4)
    in_specs = (P("parts", "rows", None), P("parts", "rows"), P(), P("parts", None, "rows", None))
    out_specs = P(("parts", "rows"), None, None, None)
    return jax.shard_map(
        functools.partial(shards, devices, members),
        mesh=mesh,
        in_specs=in_specs,
        out_specs=out_specs,
        check_vma=False,
    )
```

```python
import functools
import math

import jax
import jax.numpy as jnp
import numpy as np
from jax import lax
from jax.experimental import pallas as pl
from jax.experimental.pallas import tpu as pltpu
from jax.sharding import PartitionSpec as P


FIRST = 64
BAND = 16
F32 = jnp.float32
BF16 = jnp.bfloat16


def dot(a, b, dims=((1,), (0,)), **kw):
    return lax.dot_general(a, b, (dims, ((), ())), preferred_element_type=F32, **kw)


def split(x, parts):
    pieces = []
    for _ in range(parts):
        piece = x.astype(BF16)
        pieces.append(piece)
        x = x - piece.astype(F32)
    return pieces


def transform_tables(freqs, length, taps):
    bands = freqs // BAND
    order = FIRST + np.arange(freqs).reshape(bands, 1, BAND)
    lanes = 2 * freqs

    def wave(samples, norm):
        angle = 2.0 * np.pi * ((samples[:, None, None, None] * order) % length) / length
        re, im = np.cos(angle) * norm, -np.sin(angle) * norm
        plain = np.concatenate([re, im], axis=2).reshape(len(samples), -1)
        swapped = np.concatenate([im, re], axis=2).reshape(len(samples), -1)
        return plain, swapped

    plain, swapped = wave(np.arange(length), 1.0 / math.sqrt(length))
    main = np.concatenate([plain, swapped], axis=1)
    main[length - taps :] = 0.0
    one, _ = wave(np.arange(taps), 1.0)
    one = one.reshape(taps, bands, 2, BAND)
    resp_a = np.concatenate([one[:, :, :1], one[:, :, :1]], axis=2).reshape(taps, -1)
    resp_b = np.concatenate([-one[:, :, 1:], one[:, :, 1:]], axis=2).reshape(taps, -1)
    resp = np.concatenate([resp_a, resp_b], axis=1)
    tail = np.zeros((lanes, lanes))
    tail[:taps] = plain[length - taps :]
    return jnp.asarray(main, BF16), jnp.asarray(resp, F32), jnp.asarray(tail, BF16)


def prepare(bins, taps, width, filt, resp, tail, select, last):
    filt_parts, resp_parts = split(filt[...], 2), split(resp[...], 2)
    table = dot(
        jnp.concatenate([filt_parts[0], filt_parts[1], filt_parts[0]], axis=1),
        jnp.concatenate([resp_parts[0], resp_parts[0], resp_parts[1]], axis=0),
    )
    select[...] = jnp.zeros_like(select)
    for i, piece in enumerate(split(table, 2)):
        select[i * bins : (i + 1) * bins, :] = piece
    rows = []
    for b in range(bins):
        row = jnp.pad(filt[b : b + 1, :], ((0, 0), (0, width - taps)))
        row = jnp.broadcast_to(row, (taps, width))
        rows.append(pltpu.roll(row, 0, 1, stride=1, stride_axis=0))
    rows = jnp.concatenate(rows, axis=0)
    high, low = split(rows, 2)
    last[...] = (dot(high, tail[...]) + dot(low, tail[...])).astype(BF16)


def chunk_of(shot, band, per):
    return shot // per * per + (band + shot % per) % per


def spectra_kernel(bands, bins, taps, part, outs, *refs):
    trace, bin_of, main_hbm = refs[:3]
    first = part == 0
    main, binned, sem = refs[-3:]
    if first:
        filt, resp, tail = refs[3:6]
        out_refs, (select, last) = refs[6 : 6 + outs], refs[6 + outs : 8 + outs]
    else:
        select, last = refs[3:5]
        out_refs = refs[5 : 5 + outs]
    places = [(ref, i) for ref in out_refs for i in range(ref.shape[0])]
    step = pl.program_id(0)
    width = main.shape[1] // 2
    count = bin_of.shape[1]
    shots = binned.shape[0]
    group, _, length = trace.shape
    copy = pltpu.make_async_copy(main_hbm, main, sem)

    @pl.when(step == 0)
    def _():
        copy.start()
        column = jnp.transpose(bin_of[...].astype(F32), (1, 0))
        for shot in range(shots):
            at = part * shots + shot
            value = jnp.broadcast_to(column[:, at : at + 1], (count, width))
            binned[shot] = value.astype(BF16)
        if first:
            prepare(bins, taps, width, filt, resp, tail, select, last)
        copy.wait()

    signal = trace[...].reshape(group * count, length)
    of = binned[pl.ds(step * group, group)].reshape(group * count, width).astype(F32)
    lane = lax.broadcasted_iota(jnp.int32, (1, width), 1)
    lane_bin = jnp.where(lane < 2 * bins, lane % bins, -1).astype(F32)
    chosen = jnp.where(of == lane_bin, 1.0, 0.0).astype(BF16)
    looked = dot(chosen, select[...])
    ends = signal[:, length - width :].astype(F32)
    shift = taps
    while shift < width:
        ends = jnp.where(lane >= width - shift, ends, pltpu.roll(ends, width - shift, 1))
        shift *= 2
    every = width // taps
    ending = [
        jnp.where(of == (lane // taps + base).astype(F32), ends, 0.0).astype(BF16)
        for base in range(0, bins, every)
    ]
    ending = jnp.concatenate(ending, axis=1)
    spectrum = dot(signal, main[...])
    value = (
        spectrum[:, :width] * looked[:, :width]
        + spectrum[:, width:] * looked[:, width:]
        + dot(ending, last[...])
    )
    chunk = 2 * BAND
    per = width // chunk
    place = lax.broadcasted_iota(jnp.int32, (count, width), 1) // chunk
    for phase in range(per // group):

        @pl.when(step == phase)
        def _():
            moved = []
            for i in range(group):
                j = phase * group + i
                part = value[i * count : (i + 1) * count]
                moved.append(part if j == 0 else pltpu.roll(part, j * chunk, 1))
            for band in range(bands):
                out, at = places[band]
                result = moved[0] if phase == 0 else out[at].astype(F32)
                for i in range(group):
                    j = phase * group + i
                    if j:
                        result = jnp.where(place == (band + j) % per, moved[i], result)
                out[at] = result.astype(BF16)


def spectra_of(traces, offset_bin, filters, freqs, cuts):
    shots, count, length = traces.shape
    bins, taps = filters.shape
    bands = freqs // BAND
    width = 2 * freqs
    group = 2
    main, resp, tail = transform_tables(freqs, length, taps)
    per = width // (2 * BAND)
    made = [
        jax.ShapeDtypeStruct((width, 2 * width), BF16),
        jax.ShapeDtypeStruct((taps * bins, width), BF16),
    ]
    whole = lambda x: pl.BlockSpec(x.shape, lambda s: (0,) * len(x.shape))
    results, extra = [], None
    for part in range(shots // per):
        first = part == 0
        more = [filters, resp, tail] if first else extra
        cut = cuts[part]
        shapes = [jax.ShapeDtypeStruct((b - a, count, width), BF16) for a, b in cut]
        outs = pl.pallas_call(
            functools.partial(spectra_kernel, bands, bins, taps, part, len(cut)),
            grid=(per // group,),
            in_specs=[
                pl.BlockSpec(
                    (group, count, length),
                    functools.partial(lambda p, s: (p + s, 0, 0), part * per // group),
                ),
                whole(offset_bin),
                pl.BlockSpec(memory_space=pltpu.HBM),
            ]
            + [whole(x) for x in more],
            out_specs=[whole(x) for x in shapes] + ([whole(x) for x in made] if first else []),
            out_shape=shapes + (made if first else []),
            scratch_shapes=[
                pltpu.VMEM(main.shape, BF16),
                pltpu.VMEM((per, count, width), BF16),
                pltpu.SemaphoreType.DMA,
            ],
            compiler_params=pltpu.CompilerParams(vmem_limit_bytes=60 << 20),
            cost_estimate=pl.CostEstimate(
                flops=2 * per * count * length * 2 * width,
                bytes_accessed=per * count * length * 2,
                transcendentals=0,
            ),
            name="spectra",
        )(traces, offset_bin, main, *more)
        if first:
            extra = outs[len(cut) :]
        results.append(outs[: len(cut)])
    return results


def rows_kernel(block, head, starts, source, first, rest, sems):
    slots = first.shape[1]
    bands = head + rest.shape[0]
    device = lax.axis_index("rows")
    copies = []
    for i in range(slots):
        start = jnp.int32(0)
        for d, row in enumerate(starts):
            start = jnp.where(device == d, jnp.int32(int(row[i]) * block), start)
        column = pl.ds(pl.multiple_of(start, block), block)
        for k, (low, high, target) in enumerate(((0, head, first), (head, bands, rest))):
            copy = pltpu.make_async_copy(
                source.at[low:high, :, :, :, column], target.at[:, i], sems.at[i, k]
            )
            copy.start()
            copies.append(copy)
    for copy in copies:
        copy.wait()


def rows_for(data_matrix, starts, block, head):
    freqs, parts, rows, _ = data_matrix.shape
    bands = freqs // BAND
    slots = starts.shape[1]
    source = data_matrix.reshape(bands, BAND, parts, rows, -1)
    if block % 128:
        starts = jnp.asarray(starts)[lax.axis_index("rows")]
        pieces = [
            lax.dynamic_slice_in_dim(source, starts[i] * block, block, 4) for i in range(slots)
        ]
        both = jnp.stack(pieces, axis=1)
        return both[:head], both[head:]
    shape = (slots, BAND, parts, rows, block)
    kind = data_matrix.dtype
    return pl.pallas_call(
        functools.partial(rows_kernel, block, head, starts),
        in_specs=[pl.BlockSpec(memory_space=pltpu.HBM)],
        out_specs=[pl.BlockSpec(memory_space=pl.ANY)] * 2,
        out_shape=[
            jax.ShapeDtypeStruct((head,) + shape, kind),
            jax.ShapeDtypeStruct((bands - head,) + shape, kind),
        ],
        scratch_shapes=[pltpu.SemaphoreType.DMA((slots, 2))],
        compiler_params=pltpu.CompilerParams(vmem_limit_bytes=51 << 20),
        name="rows_for",
    )(source)


def merged(rows_in):
    columns = []
    for i in range(rows_in[0].shape[1]):
        part = jnp.concatenate([r[0, i] for r in rows_in], axis=2)
        columns.append(part.reshape(-1, part.shape[-1]))
    return columns


def merge_kernel(*refs):
    rows_in, out = refs[:-1], refs[-1]
    block = rows_in[0].shape[-1]
    for i, column in enumerate(merged(rows_in)):
        out[0, :, i * block : (i + 1) * block] = column


def merge(row_parts):
    number, pieces, _, parts, rows, block = row_parts[0].shape
    shape = (BAND * parts * rows * len(row_parts), pieces * block)
    return pl.pallas_call(
        merge_kernel,
        grid=(number,),
        in_specs=[
            pl.BlockSpec((1, pieces, BAND, parts, rows, block), lambda q: (q, 0, 0, 0, 0, 0))
        ]
        * len(row_parts),
        out_specs=pl.BlockSpec((1,) + shape, lambda q: (q, 0, 0)),
        out_shape=jax.ShapeDtypeStruct((number,) + shape, row_parts[0].dtype),
        compiler_params=pltpu.CompilerParams(vmem_limit_bytes=40 << 20),
        name="merge",
    )(*row_parts)


def predict_kernel(members, parts, slots, before, *refs):
    rows_in, refs = refs[:members], refs[members:]
    if members == 1:
        matrix = rows_in[0][0]
    else:
        columns = merged(rows_in)
        matrix = columns[0] if len(columns) == 1 else jnp.concatenate(columns, axis=1)
    spectra_in = refs[: slots * parts]
    mask_ref, fold_a, fold_b = refs[slots * parts : slots * parts + 3]
    out = refs[-1]
    spectra = [
        jnp.concatenate([spectra_in[p * slots + i][0] for p in range(parts)], axis=1)
        for i in range(slots)
    ]
    spectra = spectra[0] if slots == 1 else jnp.concatenate(spectra, axis=0)
    dests, rows, _ = out.shape
    total = dot(matrix, spectra)
    total = total.reshape(BAND, 2, rows, -1)
    acc = None
    for c, fold in enumerate((fold_a, fold_b)):
        value = total[:, c].reshape(BAND * rows, -1)
        value = jnp.where(mask_ref[...] != 0, value, 0.0)
        for piece in split(value, 2):
            term = dot(piece, fold[0])
            acc = term if acc is None else acc + term
    acc = acc.reshape(dests, BAND // dests, rows, -1)
    value = acc[:, 0]
    for i in range(1, BAND // dests):
        value = value + acc[:, i]
    if before:
        value = value + refs[-2][...].astype(F32)
    out[...] = value.astype(out.dtype)


def predict(matrix, spectra_parts, share, shots, first, part, before=None):
    if isinstance(matrix, list):
        number, _, _, _, rows, depth = matrix[0].shape
        all_rows = rows * len(matrix)
    else:
        number, wide, depth = matrix.shape
        all_rows = wide // (2 * BAND)
        matrix = [matrix]
    parts, slots = len(spectra_parts), len(spectra_parts[0])
    _, block, width = spectra_parts[0][0].shape
    cols = width * parts
    per = width // (2 * BAND)
    lanes = share * 2 * shots
    index = np.arange(cols)
    col_c, col_f = index // BAND % 2, index % BAND
    row_f = np.arange(BAND * all_rows) // all_rows
    mask = (row_f[:, None] == col_f[None, :]).astype(np.float32)
    fold_a = np.zeros((number, cols, share, 2, shots), np.float32)
    fold_b = np.zeros((number, cols, share, 2, shots), np.float32)
    for band in range(number):
        shot_at = np.zeros(shots, np.int64)
        for shot in range(shots):
            shot_at[chunk_of(shot, first + band, per)] = shot
        col_s = shot_at[part * per + index // (2 * BAND)]
        fold_a[band, index, col_f % share, col_c, col_s] = 1.0
        fold_b[band, index, col_f % share, 1 - col_c, col_s] = np.where(col_c == 1, -1.0, 1.0)
    consts = [
        jnp.asarray(mask, F32),
        jnp.asarray(fold_a.reshape(number, cols, lanes), BF16),
        jnp.asarray(fold_b.reshape(number, cols, lanes), BF16),
    ]
    dests = BAND // share
    out_spec = pl.BlockSpec((dests, all_rows, lanes), lambda q: (q, 0, 0))
    flat = [x for spectra in spectra_parts for x in spectra]
    starts = [first * (x.shape[0] > number) for x in flat]
    return pl.pallas_call(
        functools.partial(predict_kernel, len(matrix), parts, slots, before is not None),
        grid=(number,),
        in_specs=[
            pl.BlockSpec(
                (1,) + x.shape[1:], functools.partial(lambda n, q: (q,) + (0,) * n, x.ndim - 1)
            )
            for x in matrix
        ]
        + [
            pl.BlockSpec((1, block, width), functools.partial(lambda a, q: (a + q, 0, 0), a))
            for a in starts
        ]
        + [pl.BlockSpec(mask.shape, lambda q: (0, 0))]
        + [pl.BlockSpec((1, cols, lanes), lambda q: (q, 0, 0))] * 2
        + ([] if before is None else [out_spec]),
        out_specs=out_spec,
        out_shape=jax.ShapeDtypeStruct((number * dests, all_rows, lanes), BF16),
        compiler_params=pltpu.CompilerParams(vmem_limit_bytes=40 << 20),
        name="predict",
    )(*matrix, *flat, *consts, *([] if before is None else [before]))


def ring_of(length):
    return list(range(0, length, 2)) + list(range(1, length, 2))[::-1]


def shards(devices, members, traces, offset_bin, filters, data_matrix):
    shot_count, block, _ = traces.shape
    freqs, _, row_count, _ = data_matrix.shape
    lines = devices // members
    ring = ring_of(lines)
    after = {ring[i]: ring[(i + 1) % lines] for i in range(lines)}
    before = {b: a for a, b in after.items()}
    blocks = np.zeros((devices, members, lines), np.int32)
    for device in range(devices):
        line, member = divmod(device, members)
        for slot in range(lines):
            for m in range(members):
                blocks[device, m, slot] = line * members + (member ^ m)
            line = before[line]

    bands = freqs // BAND
    head = max(bands - 1, 1)
    first_parts, rest_parts = [None] * members, [None] * members

    def exchange(m):
        first, rest = rows_for(data_matrix, blocks[:, m], block, head)
        pairs = [(i, i ^ m) for i in range(devices)]
        if m:
            first = lax.ppermute(first, "rows", pairs)
            rest = lax.ppermute(rest, "rows", pairs)
        first_parts[m], rest_parts[m] = first, rest

    for m in range(members - 1, -1, -1):
        exchange(m)

    per = 2 * freqs // (2 * BAND)
    quads = shot_count // per
    cuts = [[(0, bands)]] * (quads - 1) + [[(0, head), (head, bands)] if bands > head else [(0, bands)]]
    pieces = [(p, [x]) for p, cut in enumerate(spectra_of(traces, offset_bin, filters, freqs, cuts)) for x in cut]
    step = [(i, after[i // members] * members + i % members) for i in range(devices)]
    for _ in range(lines - 1):
        for _, piece in pieces:
            piece.append(lax.ppermute(piece[-1], "rows", step))
    if block % 128:
        pieces = [(p, [jnp.concatenate(piece, axis=1)]) for p, piece in pieces]
        joined = lambda x: jnp.concatenate([x[:, i : i + 1] for i in range(lines)], axis=5)
        first_parts = [joined(x) for x in first_parts]
        rest_parts = [joined(x) for x in rest_parts]

    share = freqs // devices
    first_matrix = merge(first_parts)
    whole_pieces = [piece for _, piece in pieces[: quads - 1]]
    head_piece, rest_piece = pieces[quads - 1][1], pieces[-1][1]
    early = predict(first_matrix, whole_pieces, share, shot_count, 0, 0)
    early = predict(first_matrix, [head_piece], share, shot_count, 0, quads - 1, early)
    late = predict(rest_parts, whole_pieces + [rest_piece], share, shot_count, head, 0)
    partial_value = jnp.concatenate([early, late], axis=0)
    received = lax.all_to_all(partial_value, "rows", split_axis=0, concat_axis=0, tiled=True)
    choose = np.zeros((lines, members, members, row_count, lines, members, row_count))
    for line in range(lines):
        for member in range(members):
            for j in range(members):
                for r in range(row_count):
                    choose[line, member, member ^ j, r, line, j, r] = 1.0
    rows = devices * members * row_count
    choose = jnp.asarray(choose.reshape(rows, devices * row_count), BF16)
    final = dot(received.reshape(rows, -1), choose, ((0,), (0,)))
    return final.astype(BF16).reshape(share, 2, shot_count, devices * row_count)


def solution(mesh):
    devices = mesh.shape["rows"]
    members = math.gcd(devices, 4)
    in_specs = (P("parts", "rows", None), P("parts", "rows"), P(), P("parts", None, "rows", None))
    out_specs = P(("parts", "rows"), None, None, None)
    return jax.shard_map(
        functools.partial(shards, devices, members),
        mesh=mesh,
        in_specs=in_specs,
        out_specs=out_specs,
        check_vma=False,
    )
```

```python
import functools
import math

import jax
import jax.numpy as jnp
import numpy as np
from jax import lax
from jax.experimental import pallas as pl
from jax.experimental.pallas import tpu as pltpu
from jax.sharding import PartitionSpec as P


FIRST = 64
BAND = 16
F32 = jnp.float32
BF16 = jnp.bfloat16


def dot(a, b, dims=((1,), (0,)), **kw):
    return lax.dot_general(a, b, (dims, ((), ())), preferred_element_type=F32, **kw)


def split(x, parts):
    pieces = []
    for _ in range(parts):
        piece = x.astype(BF16)
        pieces.append(piece)
        x = x - piece.astype(F32)
    return pieces


def transform_tables(freqs, length, taps):
    bands = freqs // BAND
    order = FIRST + np.arange(freqs).reshape(bands, 1, BAND)
    lanes = 2 * freqs

    def wave(samples, norm):
        angle = 2.0 * np.pi * ((samples[:, None, None, None] * order) % length) / length
        re, im = np.cos(angle) * norm, -np.sin(angle) * norm
        plain = np.concatenate([re, im], axis=2).reshape(len(samples), -1)
        swapped = np.concatenate([im, re], axis=2).reshape(len(samples), -1)
        return plain, swapped

    plain, swapped = wave(np.arange(length), 1.0 / math.sqrt(length))
    main = np.concatenate([plain, swapped], axis=1)
    main[length - taps :] = 0.0
    one, _ = wave(np.arange(taps), 1.0)
    one = one.reshape(taps, bands, 2, BAND)
    resp_a = np.concatenate([one[:, :, :1], one[:, :, :1]], axis=2).reshape(taps, -1)
    resp_b = np.concatenate([-one[:, :, 1:], one[:, :, 1:]], axis=2).reshape(taps, -1)
    resp = np.concatenate([resp_a, resp_b], axis=1)
    tail = np.zeros((lanes, lanes))
    tail[:taps] = plain[length - taps :]
    return jnp.asarray(main, BF16), jnp.asarray(resp, F32), jnp.asarray(tail, BF16)


def prepare(bins, taps, width, filt, resp, tail, select, last):
    filt_parts, resp_parts = split(filt[...], 2), split(resp[...], 2)
    table = dot(
        jnp.concatenate([filt_parts[0], filt_parts[1], filt_parts[0]], axis=1),
        jnp.concatenate([resp_parts[0], resp_parts[0], resp_parts[1]], axis=0),
    )
    select[...] = jnp.zeros_like(select)
    for i, piece in enumerate(split(table, 2)):
        select[i * bins : (i + 1) * bins, :] = piece
    rows = []
    for b in range(bins):
        row = jnp.pad(filt[b : b + 1, :], ((0, 0), (0, width - taps)))
        row = jnp.broadcast_to(row, (taps, width))
        rows.append(pltpu.roll(row, 0, 1, stride=1, stride_axis=0))
    rows = jnp.concatenate(rows, axis=0)
    high, low = split(rows, 2)
    last[...] = (dot(high, tail[...]) + dot(low, tail[...])).astype(BF16)


def chunk_of(shot, band, per):
    return shot // per * per + (band + shot % per) % per


def spectra_kernel(bands, bins, taps, part, outs, *refs):
    trace, bin_of, main_hbm = refs[:3]
    first = part == 0
    main, binned, sem = refs[-3:]
    if first:
        filt, resp, tail = refs[3:6]
        out_refs, (select, last) = refs[6 : 6 + outs], refs[6 + outs : 8 + outs]
    else:
        select, last = refs[3:5]
        out_refs = refs[5 : 5 + outs]
    places = [(ref, i) for ref in out_refs for i in range(ref.shape[0])]
    step = pl.program_id(0)
    width = main.shape[1] // 2
    count = bin_of.shape[1]
    shots = binned.shape[0]
    group, _, length = trace.shape
    copy = pltpu.make_async_copy(main_hbm, main, sem)

    @pl.when(step == 0)
    def _():
        copy.start()
        column = jnp.transpose(bin_of[...].astype(F32), (1, 0))
        for shot in range(shots):
            at = part * shots + shot
            value = jnp.broadcast_to(column[:, at : at + 1], (count, width))
            binned[shot] = value.astype(BF16)
        if first:
            prepare(bins, taps, width, filt, resp, tail, select, last)
        copy.wait()

    signal = trace[...].reshape(group * count, length)
    of = binned[pl.ds(step * group, group)].reshape(group * count, width).astype(F32)
    lane = lax.broadcasted_iota(jnp.int32, (1, width), 1)
    lane_bin = jnp.where(lane < 2 * bins, lane % bins, -1).astype(F32)
    chosen = jnp.where(of == lane_bin, 1.0, 0.0).astype(BF16)
    looked = dot(chosen, select[...])
    ends = signal[:, length - width :].astype(F32)
    shift = taps
    while shift < width:
        ends = jnp.where(lane >= width - shift, ends, pltpu.roll(ends, width - shift, 1))
        shift *= 2
    every = width // taps
    ending = [
        jnp.where(of == (lane // taps + base).astype(F32), ends, 0.0).astype(BF16)
        for base in range(0, bins, every)
    ]
    ending = jnp.concatenate(ending, axis=1)
    spectrum = dot(signal, main[...])
    value = (
        spectrum[:, :width] * looked[:, :width]
        + spectrum[:, width:] * looked[:, width:]
        + dot(ending, last[...])
    )
    chunk = 2 * BAND
    per = width // chunk
    place = lax.broadcasted_iota(jnp.int32, (count, width), 1) // chunk
    for phase in range(per // group):

        @pl.when(step == phase)
        def _():
            moved = []
            for i in range(group):
                j = phase * group + i
                part = value[i * count : (i + 1) * count]
                moved.append(part if j == 0 else pltpu.roll(part, j * chunk, 1))
            for band in range(bands):
                out, at = places[band]
                result = moved[0] if phase == 0 else out[at].astype(F32)
                for i in range(group):
                    j = phase * group + i
                    if j:
                        result = jnp.where(place == (band + j) % per, moved[i], result)
                out[at] = result.astype(BF16)


def spectra_of(traces, offset_bin, filters, freqs, cuts):
    shots, count, length = traces.shape
    bins, taps = filters.shape
    bands = freqs // BAND
    width = 2 * freqs
    group = 2
    main, resp, tail = transform_tables(freqs, length, taps)
    per = width // (2 * BAND)
    made = [
        jax.ShapeDtypeStruct((width, 2 * width), BF16),
        jax.ShapeDtypeStruct((taps * bins, width), BF16),
    ]
    whole = lambda x: pl.BlockSpec(x.shape, lambda s: (0,) * len(x.shape))
    results, extra = [], None
    for part in range(shots // per):
        first = part == 0
        more = [filters, resp, tail] if first else extra
        cut = cuts[part]
        shapes = [jax.ShapeDtypeStruct((b - a, count, width), BF16) for a, b in cut]
        outs = pl.pallas_call(
            functools.partial(spectra_kernel, bands, bins, taps, part, len(cut)),
            grid=(per // group,),
            in_specs=[
                pl.BlockSpec(
                    (group, count, length),
                    functools.partial(lambda p, s: (p + s, 0, 0), part * per // group),
                ),
                whole(offset_bin),
                pl.BlockSpec(memory_space=pltpu.HBM),
            ]
            + [whole(x) for x in more],
            out_specs=[whole(x) for x in shapes] + ([whole(x) for x in made] if first else []),
            out_shape=shapes + (made if first else []),
            scratch_shapes=[
                pltpu.VMEM(main.shape, BF16),
                pltpu.VMEM((per, count, width), BF16),
                pltpu.SemaphoreType.DMA,
            ],
            compiler_params=pltpu.CompilerParams(vmem_limit_bytes=60 << 20),
            cost_estimate=pl.CostEstimate(
                flops=2 * per * count * length * 2 * width,
                bytes_accessed=per * count * length * 2,
                transcendentals=0,
            ),
            name="spectra",
        )(traces, offset_bin, main, *more)
        if first:
            extra = outs[len(cut) :]
        results.append(outs[: len(cut)])
    return results


def rows_kernel(block, head, starts, source, first, rest, sems):
    slots = first.shape[1]
    bands = head + rest.shape[0]
    device = lax.axis_index("rows")
    copies = []
    for i in range(slots):
        start = jnp.int32(0)
        for d, row in enumerate(starts):
            start = jnp.where(device == d, jnp.int32(int(row[i]) * block), start)
        column = pl.ds(pl.multiple_of(start, block), block)
        for k, (low, high, target) in enumerate(((0, head, first), (head, bands, rest))):
            copy = pltpu.make_async_copy(
                source.at[low:high, :, :, :, column], target.at[:, i], sems.at[i, k]
            )
            copy.start()
            copies.append(copy)
    for copy in copies:
        copy.wait()


def rows_for(data_matrix, starts, block, head):
    freqs, parts, rows, _ = data_matrix.shape
    bands = freqs // BAND
    slots = starts.shape[1]
    source = data_matrix.reshape(bands, BAND, parts, rows, -1)
    if block % 128:
        starts = jnp.asarray(starts)[lax.axis_index("rows")]
        pieces = [
            lax.dynamic_slice_in_dim(source, starts[i] * block, block, 4) for i in range(slots)
        ]
        both = jnp.stack(pieces, axis=1)
        return both[:head], both[head:]
    shape = (slots, BAND, parts, rows, block)
    kind = data_matrix.dtype
    return pl.pallas_call(
        functools.partial(rows_kernel, block, head, starts),
        in_specs=[pl.BlockSpec(memory_space=pltpu.HBM)],
        out_specs=[pl.BlockSpec(memory_space=pl.ANY)] * 2,
        out_shape=[
            jax.ShapeDtypeStruct((head,) + shape, kind),
            jax.ShapeDtypeStruct((bands - head,) + shape, kind),
        ],
        scratch_shapes=[pltpu.SemaphoreType.DMA((slots, 2))],
        compiler_params=pltpu.CompilerParams(vmem_limit_bytes=51 << 20),
        name="rows_for",
    )(source)


def merged(rows_in):
    columns = []
    for i in range(rows_in[0].shape[1]):
        part = jnp.concatenate([r[0, i] for r in rows_in], axis=2)
        columns.append(part.reshape(-1, part.shape[-1]))
    return columns


def merge_kernel(*refs):
    rows_in, out = refs[:-1], refs[-1]
    block = rows_in[0].shape[-1]
    for i, column in enumerate(merged(rows_in)):
        out[0, :, i * block : (i + 1) * block] = column


def merge(row_parts):
    number, pieces, _, parts, rows, block = row_parts[0].shape
    shape = (BAND * parts * rows * len(row_parts), pieces * block)
    return pl.pallas_call(
        merge_kernel,
        grid=(number,),
        in_specs=[
            pl.BlockSpec((1, pieces, BAND, parts, rows, block), lambda q: (q, 0, 0, 0, 0, 0))
        ]
        * len(row_parts),
        out_specs=pl.BlockSpec((1,) + shape, lambda q: (q, 0, 0)),
        out_shape=jax.ShapeDtypeStruct((number,) + shape, row_parts[0].dtype),
        compiler_params=pltpu.CompilerParams(vmem_limit_bytes=40 << 20),
        name="merge",
    )(*row_parts)


def predict_kernel(members, parts, slots, before, *refs):
    for q in range(refs[0].shape[0]):
        predict_band(members, parts, slots, before, q, *refs)


def predict_band(members, parts, slots, before, q, *refs):
    number = refs[0].shape[0]
    rows_in, refs = refs[:members], refs[members:]
    if members == 1:
        matrix = rows_in[0][q]
    else:
        columns = merged(rows_in)
        matrix = columns[0] if len(columns) == 1 else jnp.concatenate(columns, axis=1)
    spectra_in = refs[: slots * parts]
    mask_ref, fold_a, fold_b = refs[slots * parts : slots * parts + 3]
    out = refs[-1]
    spectra = [
        jnp.concatenate([spectra_in[p * slots + i][q] for p in range(parts)], axis=1)
        for i in range(slots)
    ]
    spectra = spectra[0] if slots == 1 else jnp.concatenate(spectra, axis=0)
    dests, rows, _ = out.shape
    dests //= number
    span = pl.ds(q * dests, dests)
    total = dot(matrix, spectra)
    total = total.reshape(BAND, 2, rows, -1)
    acc = None
    for c, fold in enumerate((fold_a, fold_b)):
        value = total[:, c].reshape(BAND * rows, -1)
        value = jnp.where(mask_ref[...] != 0, value, 0.0)
        for piece in split(value, 2):
            term = dot(piece, fold[q])
            acc = term if acc is None else acc + term
    acc = acc.reshape(dests, BAND // dests, rows, -1)
    value = acc[:, 0]
    for i in range(1, BAND // dests):
        value = value + acc[:, i]
    if before:
        value = value + refs[-2][span].astype(F32)
    out[span] = value.astype(out.dtype)


def predict(matrix, spectra_parts, share, shots, first, part, before=None):
    if isinstance(matrix, list):
        number, _, _, _, rows, depth = matrix[0].shape
        all_rows = rows * len(matrix)
    else:
        number, wide, depth = matrix.shape
        all_rows = wide // (2 * BAND)
        matrix = [matrix]
    parts, slots = len(spectra_parts), len(spectra_parts[0])
    _, block, width = spectra_parts[0][0].shape
    cols = width * parts
    per = width // (2 * BAND)
    lanes = share * 2 * shots
    index = np.arange(cols)
    col_c, col_f = index // BAND % 2, index % BAND
    row_f = np.arange(BAND * all_rows) // all_rows
    mask = (row_f[:, None] == col_f[None, :]).astype(np.float32)
    fold_a = np.zeros((number, cols, share, 2, shots), np.float32)
    fold_b = np.zeros((number, cols, share, 2, shots), np.float32)
    for band in range(number):
        shot_at = np.zeros(shots, np.int64)
        for shot in range(shots):
            shot_at[chunk_of(shot, first + band, per)] = shot
        col_s = shot_at[part * per + index // (2 * BAND)]
        fold_a[band, index, col_f % share, col_c, col_s] = 1.0
        fold_b[band, index, col_f % share, 1 - col_c, col_s] = np.where(col_c == 1, -1.0, 1.0)
    consts = [
        jnp.asarray(mask, F32),
        jnp.asarray(fold_a.reshape(number, cols, lanes), BF16),
        jnp.asarray(fold_b.reshape(number, cols, lanes), BF16),
    ]
    dests = BAND // share
    out_spec = pl.BlockSpec((number * dests, all_rows, lanes), lambda q: (0, 0, 0))
    flat = [x for spectra in spectra_parts for x in spectra]
    starts = [first * (x.shape[0] > number) // number for x in flat]
    return pl.pallas_call(
        functools.partial(predict_kernel, len(matrix), parts, slots, before is not None),
        grid=(1,),
        in_specs=[
            pl.BlockSpec(x.shape, functools.partial(lambda n, q: (0,) * n, x.ndim)) for x in matrix
        ]
        + [
            pl.BlockSpec((number, block, width), functools.partial(lambda a, q: (a, 0, 0), a))
            for a in starts
        ]
        + [pl.BlockSpec(mask.shape, lambda q: (0, 0))]
        + [pl.BlockSpec((number, cols, lanes), lambda q: (0, 0, 0))] * 2
        + ([] if before is None else [out_spec]),
        out_specs=out_spec,
        out_shape=jax.ShapeDtypeStruct((number * dests, all_rows, lanes), BF16),
        compiler_params=pltpu.CompilerParams(vmem_limit_bytes=40 << 20),
        name="predict",
    )(*matrix, *flat, *consts, *([] if before is None else [before]))


def ring_of(length):
    return list(range(0, length, 2)) + list(range(1, length, 2))[::-1]


def shards(devices, members, traces, offset_bin, filters, data_matrix):
    shot_count, block, _ = traces.shape
    freqs, _, row_count, _ = data_matrix.shape
    lines = devices // members
    ring = ring_of(lines)
    after = {ring[i]: ring[(i + 1) % lines] for i in range(lines)}
    before = {b: a for a, b in after.items()}
    blocks = np.zeros((devices, members, lines), np.int32)
    for device in range(devices):
        line, member = divmod(device, members)
        for slot in range(lines):
            for m in range(members):
                blocks[device, m, slot] = line * members + (member ^ m)
            line = before[line]

    bands = freqs // BAND
    head = max(bands - 1, 1)
    first_parts, rest_parts = [None] * members, [None] * members

    def exchange(m):
        first, rest = rows_for(data_matrix, blocks[:, m], block, head)
        pairs = [(i, i ^ m) for i in range(devices)]
        if m:
            first = lax.ppermute(first, "rows", pairs)
            rest = lax.ppermute(rest, "rows", pairs)
        first_parts[m], rest_parts[m] = first, rest

    for m in range(members - 1, -1, -1):
        exchange(m)

    per = 2 * freqs // (2 * BAND)
    quads = shot_count // per
    cuts = [[(0, bands)]] * (quads - 1) + [[(0, head), (head, bands)] if bands > head else [(0, bands)]]
    pieces = [(p, [x]) for p, cut in enumerate(spectra_of(traces, offset_bin, filters, freqs, cuts)) for x in cut]
    step = [(i, after[i // members] * members + i % members) for i in range(devices)]
    for _ in range(lines - 1):
        for _, piece in pieces:
            piece.append(lax.ppermute(piece[-1], "rows", step))
    if block % 128:
        pieces = [(p, [jnp.concatenate(piece, axis=1)]) for p, piece in pieces]
        joined = lambda x: jnp.concatenate([x[:, i : i + 1] for i in range(lines)], axis=5)
        first_parts = [joined(x) for x in first_parts]
        rest_parts = [joined(x) for x in rest_parts]

    share = freqs // devices
    first_matrix = merge(first_parts)
    whole_pieces = [piece for _, piece in pieces[: quads - 1]]
    head_piece, rest_piece = pieces[quads - 1][1], pieces[-1][1]
    early = predict(first_matrix, whole_pieces, share, shot_count, 0, 0)
    early = predict(first_matrix, [head_piece], share, shot_count, 0, quads - 1, early)
    late = predict(rest_parts, whole_pieces + [rest_piece], share, shot_count, head, 0)
    partial_value = jnp.concatenate([early, late], axis=0)
    received = lax.all_to_all(partial_value, "rows", split_axis=0, concat_axis=0, tiled=True)
    choose = np.zeros((lines, members, members, row_count, lines, members, row_count))
    for line in range(lines):
        for member in range(members):
            for j in range(members):
                for r in range(row_count):
                    choose[line, member, member ^ j, r, line, j, r] = 1.0
    rows = devices * members * row_count
    choose = jnp.asarray(choose.reshape(rows, devices * row_count), BF16)
    final = dot(received.reshape(rows, -1), choose, ((0,), (0,)))
    return final.astype(BF16).reshape(share, 2, shot_count, devices * row_count)


def solution(mesh):
    devices = mesh.shape["rows"]
    members = math.gcd(devices, 4)
    in_specs = (P("parts", "rows", None), P("parts", "rows"), P(), P("parts", None, "rows", None))
    out_specs = P(("parts", "rows"), None, None, None)
    return jax.shard_map(
        functools.partial(shards, devices, members),
        mesh=mesh,
        in_specs=in_specs,
        out_specs=out_specs,
        check_vma=False,
    )
```

```python
import functools
import math

import jax
import jax.numpy as jnp
import numpy as np
from jax import lax
from jax.experimental import pallas as pl
from jax.experimental.pallas import tpu as pltpu
from jax.sharding import PartitionSpec as P


FIRST = 64
BAND = 16
F32 = jnp.float32
BF16 = jnp.bfloat16


def dot(a, b, dims=((1,), (0,)), **kw):
    return lax.dot_general(a, b, (dims, ((), ())), preferred_element_type=F32, **kw)


def split(x, parts):
    pieces = []
    for _ in range(parts):
        piece = x.astype(BF16)
        pieces.append(piece)
        x = x - piece.astype(F32)
    return pieces


def transform_tables(freqs, length, taps):
    bands = freqs // BAND
    order = FIRST + np.arange(freqs).reshape(bands, 1, BAND)
    lanes = 2 * freqs

    def wave(samples, norm):
        angle = 2.0 * np.pi * ((samples[:, None, None, None] * order) % length) / length
        re, im = np.cos(angle) * norm, -np.sin(angle) * norm
        plain = np.concatenate([re, im], axis=2).reshape(len(samples), -1)
        swapped = np.concatenate([im, re], axis=2).reshape(len(samples), -1)
        return plain, swapped

    plain, swapped = wave(np.arange(length), 1.0 / math.sqrt(length))
    main = np.concatenate([plain, swapped], axis=1)
    main[length - taps :] = 0.0
    one, _ = wave(np.arange(taps), 1.0)
    one = one.reshape(taps, bands, 2, BAND)
    resp_a = np.concatenate([one[:, :, :1], one[:, :, :1]], axis=2).reshape(taps, -1)
    resp_b = np.concatenate([-one[:, :, 1:], one[:, :, 1:]], axis=2).reshape(taps, -1)
    resp = np.concatenate([resp_a, resp_b], axis=1)
    tail = np.zeros((lanes, lanes))
    tail[:taps] = plain[length - taps :]
    return jnp.asarray(main, BF16), jnp.asarray(resp, F32), jnp.asarray(tail, BF16)


def prepare(bins, taps, width, filt, resp, tail, select, last):
    filt_parts, resp_parts = split(filt[...], 2), split(resp[...], 2)
    table = dot(
        jnp.concatenate([filt_parts[0], filt_parts[1], filt_parts[0]], axis=1),
        jnp.concatenate([resp_parts[0], resp_parts[0], resp_parts[1]], axis=0),
    )
    select[...] = jnp.zeros_like(select)
    for i, piece in enumerate(split(table, 2)):
        select[i * bins : (i + 1) * bins, :] = piece
    rows = []
    for b in range(bins):
        row = jnp.pad(filt[b : b + 1, :], ((0, 0), (0, width - taps)))
        row = jnp.broadcast_to(row, (taps, width))
        rows.append(pltpu.roll(row, 0, 1, stride=1, stride_axis=0))
    rows = jnp.concatenate(rows, axis=0)
    high, low = split(rows, 2)
    last[...] = (dot(high, tail[...]) + dot(low, tail[...])).astype(BF16)


def chunk_of(shot, band, per):
    return shot // per * per + (band + shot % per) % per


def spectra_kernel(bands, bins, taps, part, outs, *refs):
    trace, bin_of, main_hbm = refs[:3]
    first = part == 0
    main, binned, sem = refs[-3:]
    if first:
        filt, resp, tail = refs[3:6]
        out_refs, (select, last) = refs[6 : 6 + outs], refs[6 + outs : 8 + outs]
    else:
        select, last = refs[3:5]
        out_refs = refs[5 : 5 + outs]
    places = [(ref, i) for ref in out_refs for i in range(ref.shape[0])]
    step = pl.program_id(0)
    width = main.shape[1] // 2
    count = bin_of.shape[1]
    shots = binned.shape[0]
    group, _, length = trace.shape
    copy = pltpu.make_async_copy(main_hbm, main, sem)

    @pl.when(step == 0)
    def _():
        copy.start()
        column = jnp.transpose(bin_of[...].astype(F32), (1, 0))
        for shot in range(shots):
            at = part * shots + shot
            value = jnp.broadcast_to(column[:, at : at + 1], (count, width))
            binned[shot] = value.astype(BF16)
        if first:
            prepare(bins, taps, width, filt, resp, tail, select, last)
        copy.wait()

    signal = trace[...].reshape(group * count, length)
    of = binned[pl.ds(step * group, group)].reshape(group * count, width).astype(F32)
    lane = lax.broadcasted_iota(jnp.int32, (1, width), 1)
    lane_bin = jnp.where(lane < 2 * bins, lane % bins, -1).astype(F32)
    chosen = jnp.where(of == lane_bin, 1.0, 0.0).astype(BF16)
    looked = dot(chosen, select[...])
    ends = signal[:, length - width :].astype(F32)
    shift = taps
    while shift < width:
        ends = jnp.where(lane >= width - shift, ends, pltpu.roll(ends, width - shift, 1))
        shift *= 2
    every = width // taps
    ending = [
        jnp.where(of == (lane // taps + base).astype(F32), ends, 0.0).astype(BF16)
        for base in range(0, bins, every)
    ]
    ending = jnp.concatenate(ending, axis=1)
    spectrum = dot(signal, main[...])
    value = (
        spectrum[:, :width] * looked[:, :width]
        + spectrum[:, width:] * looked[:, width:]
        + dot(ending, last[...])
    )
    chunk = 2 * BAND
    per = width // chunk
    place = lax.broadcasted_iota(jnp.int32, (count, width), 1) // chunk
    for phase in range(per // group):

        @pl.when(step == phase)
        def _():
            moved = []
            for i in range(group):
                j = phase * group + i
                part = value[i * count : (i + 1) * count]
                moved.append(part if j == 0 else pltpu.roll(part, j * chunk, 1))
            for band in range(bands):
                out, at = places[band]
                result = moved[0] if phase == 0 else out[at].astype(F32)
                for i in range(group):
                    j = phase * group + i
                    if j:
                        result = jnp.where(place == (band + j) % per, moved[i], result)
                out[at] = result.astype(BF16)


def spectra_of(traces, offset_bin, filters, freqs, cuts):
    shots, count, length = traces.shape
    bins, taps = filters.shape
    bands = freqs // BAND
    width = 2 * freqs
    group = 4
    main, resp, tail = transform_tables(freqs, length, taps)
    per = width // (2 * BAND)
    made = [
        jax.ShapeDtypeStruct((width, 2 * width), BF16),
        jax.ShapeDtypeStruct((taps * bins, width), BF16),
    ]
    whole = lambda x: pl.BlockSpec(x.shape, lambda s: (0,) * len(x.shape))
    results, extra = [], None
    for part in range(shots // per):
        first = part == 0
        more = [filters, resp, tail] if first else extra
        cut = cuts[part]
        shapes = [jax.ShapeDtypeStruct((b - a, count, width), BF16) for a, b in cut]
        outs = pl.pallas_call(
            functools.partial(spectra_kernel, bands, bins, taps, part, len(cut)),
            grid=(per // group,),
            in_specs=[
                pl.BlockSpec(
                    (group, count, length),
                    functools.partial(lambda p, s: (p + s, 0, 0), part * per // group),
                ),
                whole(offset_bin),
                pl.BlockSpec(memory_space=pltpu.HBM),
            ]
            + [whole(x) for x in more],
            out_specs=[whole(x) for x in shapes] + ([whole(x) for x in made] if first else []),
            out_shape=shapes + (made if first else []),
            scratch_shapes=[
                pltpu.VMEM(main.shape, BF16),
                pltpu.VMEM((per, count, width), BF16),
                pltpu.SemaphoreType.DMA,
            ],
            compiler_params=pltpu.CompilerParams(vmem_limit_bytes=60 << 20),
            cost_estimate=pl.CostEstimate(
                flops=2 * per * count * length * 2 * width,
                bytes_accessed=per * count * length * 2,
                transcendentals=0,
            ),
            name="spectra",
        )(traces, offset_bin, main, *more)
        if first:
            extra = outs[len(cut) :]
        results.append(outs[: len(cut)])
    return results


def rows_kernel(block, head, starts, source, first, rest, sems):
    slots = first.shape[1]
    bands = head + rest.shape[0]
    device = lax.axis_index("rows")
    copies = []
    for i in range(slots):
        start = jnp.int32(0)
        for d, row in enumerate(starts):
            start = jnp.where(device == d, jnp.int32(int(row[i]) * block), start)
        column = pl.ds(pl.multiple_of(start, block), block)
        for k, (low, high, target) in enumerate(((0, head, first), (head, bands, rest))):
            copy = pltpu.make_async_copy(
                source.at[low:high, :, :, :, column], target.at[:, i], sems.at[i, k]
            )
            copy.start()
            copies.append(copy)
    for copy in copies:
        copy.wait()


def rows_for(data_matrix, starts, block, head):
    freqs, parts, rows, _ = data_matrix.shape
    bands = freqs // BAND
    slots = starts.shape[1]
    source = data_matrix.reshape(bands, BAND, parts, rows, -1)
    if block % 128:
        starts = jnp.asarray(starts)[lax.axis_index("rows")]
        pieces = [
            lax.dynamic_slice_in_dim(source, starts[i] * block, block, 4) for i in range(slots)
        ]
        both = jnp.stack(pieces, axis=1)
        return both[:head], both[head:]
    shape = (slots, BAND, parts, rows, block)
    kind = data_matrix.dtype
    return pl.pallas_call(
        functools.partial(rows_kernel, block, head, starts),
        in_specs=[pl.BlockSpec(memory_space=pltpu.HBM)],
        out_specs=[pl.BlockSpec(memory_space=pl.ANY)] * 2,
        out_shape=[
            jax.ShapeDtypeStruct((head,) + shape, kind),
            jax.ShapeDtypeStruct((bands - head,) + shape, kind),
        ],
        scratch_shapes=[pltpu.SemaphoreType.DMA((slots, 2))],
        compiler_params=pltpu.CompilerParams(vmem_limit_bytes=51 << 20),
        name="rows_for",
    )(source)


def merged(rows_in):
    columns = []
    for i in range(rows_in[0].shape[1]):
        part = jnp.concatenate([r[0, i] for r in rows_in], axis=2)
        columns.append(part.reshape(-1, part.shape[-1]))
    return columns


def merge_kernel(*refs):
    rows_in, out = refs[:-1], refs[-1]
    block = rows_in[0].shape[-1]
    for i, column in enumerate(merged(rows_in)):
        out[0, :, i * block : (i + 1) * block] = column


def merge(row_parts):
    number, pieces, _, parts, rows, block = row_parts[0].shape
    shape = (BAND * parts * rows * len(row_parts), pieces * block)
    return pl.pallas_call(
        merge_kernel,
        grid=(number,),
        in_specs=[
            pl.BlockSpec((1, pieces, BAND, parts, rows, block), lambda q: (q, 0, 0, 0, 0, 0))
        ]
        * len(row_parts),
        out_specs=pl.BlockSpec((1,) + shape, lambda q: (q, 0, 0)),
        out_shape=jax.ShapeDtypeStruct((number,) + shape, row_parts[0].dtype),
        compiler_params=pltpu.CompilerParams(vmem_limit_bytes=40 << 20),
        name="merge",
    )(*row_parts)


def predict_kernel(members, parts, slots, before, *refs):
    for q in range(refs[0].shape[0]):
        predict_band(members, parts, slots, before, q, *refs)


def predict_band(members, parts, slots, before, q, *refs):
    number = refs[0].shape[0]
    rows_in, refs = refs[:members], refs[members:]
    if len(rows_in[0].shape) == 3:
        matrix = rows_in[0][q]
    else:
        columns = merged(rows_in)
        matrix = columns[0] if len(columns) == 1 else jnp.concatenate(columns, axis=1)
    spectra_in = refs[: slots * parts]
    mask_ref, fold_a, fold_b = refs[slots * parts : slots * parts + 3]
    out = refs[-1]
    spectra = [
        jnp.concatenate([spectra_in[p * slots + i][q] for p in range(parts)], axis=1)
        for i in range(slots)
    ]
    spectra = spectra[0] if slots == 1 else jnp.concatenate(spectra, axis=0)
    dests, rows, _ = out.shape
    dests //= number
    span = pl.ds(q * dests, dests)
    total = dot(matrix, spectra)
    total = total.reshape(BAND, 2, rows, -1)
    acc = None
    for c, fold in enumerate((fold_a, fold_b)):
        value = total[:, c].reshape(BAND * rows, -1)
        value = jnp.where(mask_ref[...] != 0, value, 0.0)
        for piece in split(value, 2):
            term = dot(piece, fold[q])
            acc = term if acc is None else acc + term
    acc = acc.reshape(dests, BAND // dests, rows, -1)
    value = acc[:, 0]
    for i in range(1, BAND // dests):
        value = value + acc[:, i]
    if before:
        value = value + refs[-2][span].astype(F32)
    out[span] = value.astype(out.dtype)


def predict(matrix, spectra_parts, share, shots, first, part, before=None):
    if isinstance(matrix, list):
        number, _, _, _, rows, depth = matrix[0].shape
        all_rows = rows * len(matrix)
    else:
        number, wide, depth = matrix.shape
        all_rows = wide // (2 * BAND)
        matrix = [matrix]
    parts, slots = len(spectra_parts), len(spectra_parts[0])
    _, block, width = spectra_parts[0][0].shape
    cols = width * parts
    per = width // (2 * BAND)
    lanes = share * 2 * shots
    index = np.arange(cols)
    col_c, col_f = index // BAND % 2, index % BAND
    row_f = np.arange(BAND * all_rows) // all_rows
    mask = (row_f[:, None] == col_f[None, :]).astype(np.float32)
    fold_a = np.zeros((number, cols, share, 2, shots), np.float32)
    fold_b = np.zeros((number, cols, share, 2, shots), np.float32)
    for band in range(number):
        shot_at = np.zeros(shots, np.int64)
        for shot in range(shots):
            shot_at[chunk_of(shot, first + band, per)] = shot
        col_s = shot_at[part * per + index // (2 * BAND)]
        fold_a[band, index, col_f % share, col_c, col_s] = 1.0
        fold_b[band, index, col_f % share, 1 - col_c, col_s] = np.where(col_c == 1, -1.0, 1.0)
    consts = [
        jnp.asarray(mask, F32),
        jnp.asarray(fold_a.reshape(number, cols, lanes), BF16),
        jnp.asarray(fold_b.reshape(number, cols, lanes), BF16),
    ]
    dests = BAND // share
    out_spec = pl.BlockSpec((number * dests, all_rows, lanes), lambda q: (0, 0, 0))
    flat = [x for spectra in spectra_parts for x in spectra]
    starts = [first * (x.shape[0] > number) // number for x in flat]
    return pl.pallas_call(
        functools.partial(predict_kernel, len(matrix), parts, slots, before is not None),
        grid=(1,),
        in_specs=[
            pl.BlockSpec(x.shape, functools.partial(lambda n, q: (0,) * n, x.ndim)) for x in matrix
        ]
        + [
            pl.BlockSpec((number, block, width), functools.partial(lambda a, q: (a, 0, 0), a))
            for a in starts
        ]
        + [pl.BlockSpec(mask.shape, lambda q: (0, 0))]
        + [pl.BlockSpec((number, cols, lanes), lambda q: (0, 0, 0))] * 2
        + ([] if before is None else [out_spec]),
        out_specs=out_spec,
        out_shape=jax.ShapeDtypeStruct((number * dests, all_rows, lanes), BF16),
        compiler_params=pltpu.CompilerParams(vmem_limit_bytes=40 << 20),
        name="predict",
    )(*matrix, *flat, *consts, *([] if before is None else [before]))


def ring_of(length):
    return list(range(0, length, 2)) + list(range(1, length, 2))[::-1]


def shards(devices, members, traces, offset_bin, filters, data_matrix):
    shot_count, block, _ = traces.shape
    freqs, _, row_count, _ = data_matrix.shape
    lines = devices // members
    ring = ring_of(lines)
    after = {ring[i]: ring[(i + 1) % lines] for i in range(lines)}
    before = {b: a for a, b in after.items()}
    blocks = np.zeros((devices, members, lines), np.int32)
    for device in range(devices):
        line, member = divmod(device, members)
        for slot in range(lines):
            for m in range(members):
                blocks[device, m, slot] = line * members + (member ^ m)
            line = before[line]

    bands = freqs // BAND
    head = max(bands - 1, 1)
    first_parts, rest_parts = [None] * members, [None] * members

    def exchange(m):
        first, rest = rows_for(data_matrix, blocks[:, m], block, head)
        pairs = [(i, i ^ m) for i in range(devices)]
        if m:
            first = lax.ppermute(first, "rows", pairs)
            rest = lax.ppermute(rest, "rows", pairs)
        first_parts[m], rest_parts[m] = first, rest

    for m in range(members - 1, -1, -1):
        exchange(m)

    per = 2 * freqs // (2 * BAND)
    quads = shot_count // per
    cuts = [[(0, bands)]] * (quads - 1) + [[(0, head), (head, bands)] if bands > head else [(0, bands)]]
    pieces = [(p, [x]) for p, cut in enumerate(spectra_of(traces, offset_bin, filters, freqs, cuts)) for x in cut]
    step = [(i, after[i // members] * members + i % members) for i in range(devices)]
    for _ in range(lines - 1):
        for _, piece in pieces:
            piece.append(lax.ppermute(piece[-1], "rows", step))
    if block % 128:
        pieces = [(p, [jnp.concatenate(piece, axis=1)]) for p, piece in pieces]
        joined = lambda x: jnp.concatenate([x[:, i : i + 1] for i in range(lines)], axis=5)
        first_parts = [joined(x) for x in first_parts]
        rest_parts = [joined(x) for x in rest_parts]

    share = freqs // devices
    first_matrix = merge(first_parts)
    whole_pieces = [piece for _, piece in pieces[: quads - 1]]
    head_piece, rest_piece = pieces[quads - 1][1], pieces[-1][1]
    early = predict(first_matrix, whole_pieces, share, shot_count, 0, 0)
    early = predict(first_matrix, [head_piece], share, shot_count, 0, quads - 1, early)
    absent = members // 2
    others = [x for m, x in enumerate(rest_parts) if m != absent or members == 1]
    late = predict(others, whole_pieces + [rest_piece], share, shot_count, head, 0)
    if len(others) < members:
        last = predict([rest_parts[absent]], whole_pieces + [rest_piece], share, shot_count, head, 0)
        at = absent * row_count
        late = jnp.concatenate([late[:, :at], last, late[:, at:]], axis=1)
    partial_value = jnp.concatenate([early, late], axis=0)
    received = lax.all_to_all(partial_value, "rows", split_axis=0, concat_axis=0, tiled=True)
    choose = np.zeros((lines, members, members, row_count, lines, members, row_count))
    for line in range(lines):
        for member in range(members):
            for j in range(members):
                for r in range(row_count):
                    choose[line, member, member ^ j, r, line, j, r] = 1.0
    rows = devices * members * row_count
    choose = jnp.asarray(choose.reshape(rows, devices * row_count), BF16)
    final = dot(received.reshape(rows, -1), choose, ((0,), (0,)))
    return final.astype(BF16).reshape(share, 2, shot_count, devices * row_count)


def solution(mesh):
    devices = mesh.shape["rows"]
    members = math.gcd(devices, 4)
    in_specs = (P("parts", "rows", None), P("parts", "rows"), P(), P("parts", None, "rows", None))
    out_specs = P(("parts", "rows"), None, None, None)
    return jax.shard_map(
        functools.partial(shards, devices, members),
        mesh=mesh,
        in_specs=in_specs,
        out_specs=out_specs,
        check_vma=False,
    )
```
